768 devices in a mesh: space: 24 (over z, y_hi), tp: 32 (over y_lo, x, core).
Axes of the slice: x: 4, y: 8 (y_hi: 2, y_lo: 4; y = y_hi * 4 + y_lo), z: 12, core: 2. Of those that a mesh axis runs over, the one named last changes fastest.
Arguments:
- queries: bfloat16 [192, 128, 4, 1024], P('space', 'tp'), may hold values from -9.7 to 9.7
- key_field: bfloat16 [192, 128, 4, 1024], P('space', 'tp'), may hold values from -4 to 4
- value_field: bfloat16 [192, 128, 4, 1024], P('space', 'tp'), may hold values from -12 to 12
- upstream: bfloat16 [192, 128, 4, 1024], P('space', 'tp'), may hold values from -6 to 6
Outputs:
- out: bfloat16 [192, 128, 4, 1024], P('space', 'tp')
- grad_queries: bfloat16 [192, 128, 4, 1024], P('space', 'tp')
- grad_keys: bfloat16 [192, 128, 4, 1024], P('space', 'tp')
- grad_values: bfloat16 [192, 128, 4, 1024], P('space', 'tp')
The draws below stay inside these ranges and needn't reach their ends.
All inputs are finite; a program needn't handle non-finite values.
Results may differ from the reference program's by a relative error of at most 0.0093.
Values may be sent and summed in bfloat16 or wider, within the bound.
No kernel may reach another device: no remote copies, remote signals or barrier semaphores. Data moves between devices by JAX's collectives and lax.ppermute only.
A program may use at most 32 MiB of HBM per device.

```python
import math
import jax
import jax.numpy as jnp
from jax import lax

D = 1024
HEADS = 16
RADIUS = 3
CX = 8
CY = 4
GZ = 4
GX = 192
GY = 128


def draw_queries(key, part):
    drawn = jax.random.truncated_normal(jax.random.fold_in(key, 11), -4.0, 4.0, (GX, GY, GZ, D), jnp.float32)
    return drawn.astype(jnp.bfloat16)


def draw_key_field(key, part):
    drawn = jax.random.truncated_normal(jax.random.fold_in(key, 13), -4.0, 4.0, (GX, GY, GZ, D), jnp.float32)
    return drawn.astype(jnp.bfloat16)


def steps_of(rng, shape, shards, low, top_value):
    gain, own = 1.0, jax.random.fold_in(rng, 6)
    for dim, shards_of in shards:
        heights = jnp.exp(jax.random.uniform(jax.random.fold_in(own, dim), (shards_of,), jnp.float32, low / len(shards), top_value / len(shards)))
        gain = gain * jnp.repeat(heights, shape[dim] // shards_of).reshape([-1 if axis == dim else 1 for axis in range(len(shape))])
    return gain


def scatter_about(rng, shape, width, bound, shards=(), kind=jnp.bfloat16):
    entries = width * jax.random.normal(rng, shape, jnp.float32)
    if shards:
        entries = entries * steps_of(rng, shape, shards, -0.22, 0.18)
    return jnp.clip(entries, -bound, bound).astype(kind)


def setup_inputs(seed: int = 0) -> dict:
    arg_keys = jax.random.split(jax.random.key(seed), 5)
    return {
        "queries": draw_queries(jax.random.fold_in(arg_keys[4], 71), 0),
        "key_field": draw_key_field(jax.random.fold_in(arg_keys[4], 71), 0),
        "value_field": scatter_about(arg_keys[2], (GX, GY, GZ, D), 2.0, 12.0, ((0, 24), (1, 32))),
        "upstream": scatter_about(arg_keys[3], (GX, GY, GZ, D), 1.0, 6.0, ((0, 24), (1, 32))),
    }


blocked_score = -1e+30
heads_group = 4

def window_mask(along_x, along_y, depth_z, first_x, first_y, grid_x, grid_y, rim_width):
    centre_x, centre_y, centre_z = jnp.meshgrid(jnp.arange(along_x, dtype=jnp.int32), jnp.arange(along_y, dtype=jnp.int32), jnp.arange(depth_z, dtype=jnp.int32), indexing='ij')
    other_x, other_y, other_z = jnp.meshgrid(jnp.arange(along_x + 2 * rim_width, dtype=jnp.int32), jnp.arange(along_y + 2 * rim_width, dtype=jnp.int32), jnp.arange(depth_z, dtype=jnp.int32), indexing='ij')
    centre_x = centre_x.reshape(-1)[:, None]
    centre_y = centre_y.reshape(-1)[:, None]
    centre_z = centre_z.reshape(-1)[:, None]
    other_x = other_x.reshape(-1)[None, :]
    other_y = other_y.reshape(-1)[None, :]
    other_z = other_z.reshape(-1)[None, :]
    within = (jnp.abs(other_x - centre_x - rim_width) <= rim_width) & (jnp.abs(other_y - centre_y - rim_width) <= rim_width) & (jnp.abs(other_z - centre_z) <= rim_width)
    global_x = first_x + other_x - rim_width
    global_y = first_y + other_y - rim_width
    inside = (global_x >= 0) & (global_x < grid_x) & (global_y >= 0) & (global_y < grid_y)
    return within & inside

def take_heads(matrix, group_index, group_width):
    part = lax.dynamic_slice_in_dim(matrix, group_index * group_width, group_width, 1)
    return part.reshape(matrix.shape[0], heads_group, -1).astype(jnp.float32)

def take_stats(matrix, group_index):
    return jnp.transpose(lax.dynamic_slice_in_dim(matrix, group_index * heads_group, heads_group, 1))

def regroup(stacked):
    groups, row_total, group_width = stacked.shape
    return jnp.transpose(stacked, (1, 0, 2)).reshape(row_total, groups * group_width)

def regroup_heads(stacked):
    groups, per_group, row_total = stacked.shape
    return jnp.transpose(stacked, (2, 0, 1)).reshape(row_total, groups * per_group)

def rounded(values_in):
    return lax.optimization_barrier(values_in.astype(jnp.bfloat16)).astype(jnp.float32)

def attend_forward(centre_q, other_k, other_v, allowed, head_size):
    row_total = centre_q.shape[0]
    group_width = heads_group * head_size
    inv_root = 1.0 / math.sqrt(head_size)

    def one_group(group_index):
        query_part = take_heads(centre_q, group_index, group_width)
        key_part = take_heads(other_k, group_index, group_width)
        value_part = take_heads(other_v, group_index, group_width)
        scores = jnp.einsum('qhd,khd->hqk', query_part, key_part) * inv_root
        scores = jnp.where(allowed[None], scores, blocked_score)
        highest = lax.optimization_barrier(jnp.max(scores, axis=2, keepdims=True))
        summed = lax.optimization_barrier(jnp.sum(jnp.exp(scores - highest), axis=2, keepdims=True))
        log_total = highest + jnp.log(summed)
        weights = rounded(jnp.exp(scores - log_total))
        attended = jnp.einsum('hqk,khd->qhd', weights, value_part).astype(jnp.bfloat16)
        return (attended.reshape(row_total, group_width), log_total[:, :, 0])
    attended, log_total = lax.map(one_group, jnp.arange(HEADS // heads_group, dtype=jnp.int32))
    return (regroup(attended), regroup_heads(log_total))

def attend_queries(centre_q, centre_up, centre_lse, centre_dots, other_k, other_v, allowed, head_size):
    row_total = centre_q.shape[0]
    group_width = heads_group * head_size
    inv_root = 1.0 / math.sqrt(head_size)

    def one_group(group_index):
        up_part = take_heads(centre_up, group_index, group_width)
        query_part = take_heads(centre_q, group_index, group_width)
        key_part = take_heads(other_k, group_index, group_width)
        value_part = take_heads(other_v, group_index, group_width)
        lse_part = take_stats(centre_lse, group_index)
        dot_part = take_stats(centre_dots, group_index)
        scores = jnp.einsum('qhd,khd->hqk', query_part, key_part) * inv_root
        scores = jnp.where(allowed[None], scores, blocked_score)
        exact_prob = jnp.exp(scores - lse_part[:, :, None])
        d_prob = jnp.einsum('qhd,khd->hqk', up_part, value_part)
        dscore = rounded(exact_prob * (d_prob - dot_part[:, :, None]))
        grad_q = (jnp.einsum('hqk,khd->qhd', dscore, key_part) * inv_root).astype(jnp.bfloat16)
        return grad_q.reshape(row_total, group_width)
    return regroup(lax.map(one_group, jnp.arange(HEADS // heads_group, dtype=jnp.int32)))

def attend_keys(centre_k, centre_v, other_q, other_up, other_lse, other_dots, allowed, head_size):
    row_total = centre_k.shape[0]
    group_width = heads_group * head_size
    inv_root = 1.0 / math.sqrt(head_size)

    def one_group(group_index):
        key_part = take_heads(centre_k, group_index, group_width)
        value_part = take_heads(centre_v, group_index, group_width)
        query_part = take_heads(other_q, group_index, group_width)
        up_part = take_heads(other_up, group_index, group_width)
        lse_part = take_stats(other_lse, group_index)
        dot_part = take_stats(other_dots, group_index)
        scores = jnp.einsum('khd,qhd->hkq', key_part, query_part) * inv_root
        scores = jnp.where(allowed[None], scores, blocked_score)
        exact_prob = jnp.exp(scores - lse_part[:, None, :])
        weights = rounded(exact_prob)
        d_prob = jnp.einsum('khd,qhd->hkq', value_part, up_part)
        dscore = rounded(exact_prob * (d_prob - dot_part[:, None, :]))
        grad_k = (jnp.einsum('hkq,qhd->khd', dscore, query_part) * inv_root).astype(jnp.bfloat16)
        grad_v = jnp.einsum('hkq,qhd->khd', weights, up_part).astype(jnp.bfloat16)
        return (grad_k.reshape(row_total, group_width), grad_v.reshape(row_total, group_width))
    grad_k, grad_v = lax.map(one_group, jnp.arange(HEADS // heads_group, dtype=jnp.int32))
    return (regroup(grad_k), regroup(grad_v))

def head_products(flat_up, attended, head_count):
    fixed = lax.optimization_barrier(attended).astype(jnp.float32)
    product = flat_up.astype(jnp.float32) * fixed
    return product.reshape(product.shape[0], head_count, -1).sum(axis=2)

def reference(queries, key_field, value_field, upstream):
    grid_x, grid_y, depth_z, features = queries.shape
    head_size = features // HEADS
    blocks_x = grid_x // CX
    blocks_y = grid_y // CY
    span_x = CX + 2 * RADIUS
    span_y = CY + 2 * RADIUS
    row_total = CX * CY * depth_z
    others = span_x * span_y * depth_z
    padding = ((RADIUS, RADIUS), (RADIUS, RADIUS), (0, 0), (0, 0))

    def corner(block_id):
        start_x = (block_id // blocks_y).astype(jnp.int32) * CX
        start_y = (block_id % blocks_y).astype(jnp.int32) * CY
        return (start_x, start_y)

    def centre_of(field, block_id):
        start_x, start_y = corner(block_id)
        zero = jnp.zeros((), jnp.int32)
        piece_out = lax.dynamic_slice(field, (start_x, start_y, zero, zero), (CX, CY, depth_z, field.shape[3]))
        return piece_out.reshape(row_total, field.shape[3])

    def beside_all(padded, block_id):
        start_x, start_y = corner(block_id)
        zero = jnp.zeros((), jnp.int32)
        piece_out = lax.dynamic_slice(padded, (start_x, start_y, zero, zero), (span_x, span_y, depth_z, padded.shape[3]))
        return piece_out.reshape(others, padded.shape[3])

    def block_mask(block_id):
        start_x, start_y = corner(block_id)
        return window_mask(CX, CY, depth_z, start_x, start_y, grid_x, grid_y, RADIUS)

    def assemble(stacked):
        last_dim = stacked.shape[-1]
        shaped = stacked.reshape(blocks_x, blocks_y, CX, CY, depth_z, last_dim)
        return jnp.transpose(shaped, (0, 2, 1, 3, 4, 5)).reshape(grid_x, grid_y, depth_z, last_dim)
    block_ids = jnp.arange(blocks_x * blocks_y, dtype=jnp.int32)
    padded_k = jnp.pad(key_field, padding)
    padded_v = jnp.pad(value_field, padding)

    def forward_block(block_id):
        return attend_forward(centre_of(queries, block_id), beside_all(padded_k, block_id), beside_all(padded_v, block_id), block_mask(block_id), head_size)
    attended, log_total = lax.map(forward_block, block_ids)
    out = assemble(attended)
    lse_field = assemble(log_total)
    dot_field = head_products(upstream.reshape(-1, features), out.reshape(-1, features), HEADS).reshape(grid_x, grid_y, depth_z, HEADS)

    def query_block(block_id):
        return attend_queries(centre_of(queries, block_id), centre_of(upstream, block_id), centre_of(lse_field, block_id), centre_of(dot_field, block_id), beside_all(padded_k, block_id), beside_all(padded_v, block_id), block_mask(block_id), head_size)
    grad_queries = assemble(lax.map(query_block, block_ids))
    padded_q = jnp.pad(queries, padding)
    padded_up = jnp.pad(upstream, padding)
    padded_lse = jnp.pad(lse_field, padding)
    padded_dots = jnp.pad(dot_field, padding)

    def key_block(block_id):
        return attend_keys(centre_of(key_field, block_id), centre_of(value_field, block_id), beside_all(padded_q, block_id), beside_all(padded_up, block_id), beside_all(padded_lse, block_id), beside_all(padded_dots, block_id), block_mask(block_id), head_size)
    grad_k, grad_v = lax.map(key_block, block_ids)
    return (out, grad_queries, assemble(grad_k), assemble(grad_v))
```

```python
import math

import numpy as np
import jax
import jax.numpy as jnp
from jax import lax
from jax.experimental import pallas as pl
from jax.experimental.pallas import tpu as pltpu
from jax.sharding import PartitionSpec as P

HEADS = 16
RADIUS = 3
BLOCKED = -1e30

GROUP = 4
SIDE = 48
RIM = 3 * SIDE
CORE = 320
SPAN = CORE + RIM
FULL = CORE + 2 * RIM


def by_contract(a, b, dims):
    return lax.dot_general(a, b, (dims, ((), ())), preferred_element_type=jnp.float32)


def shift(x, axis, by):
    peers = lax.axis_size(axis)
    pairs = [(i, i + by) for i in range(peers) if 0 <= i + by < peers]
    return lax.ppermute(x, axis, pairs)


def block_diagonal(rows, scale=None):
    count, width = rows.shape
    if scale is not None:
        rows = rows * jnp.asarray(scale, rows.dtype)
    tiled = jnp.concatenate([rows] * GROUP, axis=0)
    own = lax.broadcasted_iota(jnp.int32, tiled.shape, 0) // count
    head = lax.broadcasted_iota(jnp.int32, tiled.shape, 1) // (width // GROUP)
    return jnp.where(own == head, tiled, jnp.zeros_like(tiled))


def diagonal_of(product, count):
    width = product.shape[1]
    head = lax.broadcasted_iota(jnp.int32, (count, width), 1) // (width // GROUP)
    total = product[0:count]
    for h in range(1, GROUP):
        total = jnp.where(head == h, product[h * count : (h + 1) * count], total)
    return total


def forward_kernel(
    scale,
    q_ref, u_ref, k_ref, v_ref, cl_ref, cr_ref, rlo_ref, rhi_ref, rl_ref, rr_ref, bias_ref,
    out_ref, dq_ref, lse_ref, dot_ref, dk_ref, dv_ref,
    kbuf, vbuf,
):
    @pl.when(pl.program_id(0) == 0)
    def _():
        kbuf[...] = jnp.zeros_like(kbuf)
        vbuf[...] = jnp.zeros_like(vbuf)

    for buf, own, part in ((kbuf, k_ref, 0), (vbuf, v_ref, 1)):
        buf[RIM : RIM + 96] = cl_ref[part]
        buf[RIM + 96 : RIM + 224] = own[...]
        buf[RIM + 224 : RIM + 320] = cr_ref[part]
        for side, rim_ref in ((0, rlo_ref), (1, rhi_ref)):
            base = side * (RIM + CORE)
            buf[base : base + SIDE] = rim_ref[part]
            buf[base + SIDE : base + SIDE + 36] = rl_ref[side, part]
            buf[base + 2 * SIDE : base + 2 * SIDE + 36] = rr_ref[side, part]

    for half in range(2):
        keys = kbuf[half * RIM : half * RIM + SPAN]
        vals = vbuf[half * RIM : half * RIM + SPAN]
        core = RIM * (1 - half)
        query = block_diagonal(q_ref[64 * half : 64 * half + 64], scale)
        up = block_diagonal(u_ref[64 * half : 64 * half + 64])
        scores = by_contract(keys, query, ((1,), (1,))) + bias_ref[half]
        highest = jnp.max(scores, axis=0, keepdims=True)
        prob = jnp.exp(scores - highest)
        summed = jnp.sum(prob, axis=0, keepdims=True)
        prob = prob * (1.0 / summed)
        weights = prob.astype(jnp.bfloat16)
        d_prob = by_contract(vals, up, ((1,), (1,)))
        dots = jnp.sum(weights.astype(jnp.float32) * d_prob, axis=0, keepdims=True)
        d_score = (prob * (d_prob - dots)).astype(jnp.bfloat16)
        lse_ref[half, 0] = highest + jnp.log(summed)
        dot_ref[half, 0] = dots
        out = by_contract(weights, vals, ((0,), (0,)))
        out_ref[64 * half : 64 * half + 64] = diagonal_of(out, 64).astype(jnp.bfloat16)
        grad_q = by_contract(d_score, keys, ((0,), (0,)))
        dq_ref[64 * half : 64 * half + 64] = (diagonal_of(grad_q, 64) * scale).astype(jnp.bfloat16)
        part_k = by_contract(d_score[core : core + CORE], query, ((1,), (0,)))
        part_v = by_contract(weights[core : core + CORE], up, ((1,), (0,)))
        if half == 0:
            dk_ref[...] = part_k
            dv_ref[...] = part_v
        else:
            dk_ref[...] += part_k
            dv_ref[...] += part_v


def rim_kernel(
    scale,
    qlo_ref, qhi_ref, llo_ref, dlo_ref, lhi_ref, dhi_ref, k_ref, v_ref, cl_ref, cr_ref, bias_ref, dk_ref, dv_ref,
    own_ref, left_ref, right_ref,
):
    sides = ((qlo_ref, llo_ref, dlo_ref), (qhi_ref, lhi_ref, dhi_ref))
    for side, (rows_ref, lse_ref, dot_ref) in enumerate(sides):
        left = slice(48 * side, 48 * side + 48)
        mid = slice(64 * side, 64 * side + 64)
        keys = jnp.concatenate([cl_ref[0, left], k_ref[mid], cr_ref[0, left]], axis=0)
        vals = jnp.concatenate([cl_ref[1, left], v_ref[mid], cr_ref[1, left]], axis=0)
        blank = jnp.zeros((16, keys.shape[1]), jnp.bfloat16)
        order = (lambda x: [blank, x]) if side == 0 else (lambda x: [x, blank])
        query = block_diagonal(jnp.concatenate(order(rows_ref[0]), axis=0), scale)
        up = block_diagonal(jnp.concatenate(order(rows_ref[1]), axis=0))
        scores = by_contract(keys, query, ((1,), (1,))) + bias_ref[side]
        prob = jnp.exp(scores - lse_ref[0])
        weights = prob.astype(jnp.bfloat16)
        d_prob = by_contract(vals, up, ((1,), (1,)))
        d_score = (prob * (d_prob - dot_ref[0])).astype(jnp.bfloat16)
        parts = (
            (0, dk_ref, by_contract(d_score, query, ((1,), (0,)))),
            (1, dv_ref, by_contract(weights, up, ((1,), (0,)))),
        )
        for which, sum_ref, extra in parts:
            lo, hi = 96 + 64 * side, 160 + 64 * side
            right = slice(224 + 48 * side, 272 + 48 * side)
            left_ref[which, left] = (sum_ref[left] + extra[0:48]).astype(jnp.bfloat16)
            own_ref[which, mid] = sum_ref[lo:hi] + extra[48:112]
            right_ref[which, left] = (sum_ref[right] + extra[112:160]).astype(jnp.bfloat16)


def cells(xs, ys, depth):
    x, y, _ = np.meshgrid(np.asarray(xs), np.asarray(ys), np.arange(depth), indexing="ij")
    return np.stack([x.reshape(-1), y.reshape(-1)])


def bias_of(key_cells, query_cells, first_x, first_y, grid_x, grid_y):
    apart = np.abs(key_cells[:, :, None] - query_cells[:, None, :])
    near = jnp.asarray((apart <= RADIUS).all(axis=0))

    def inside(cell):
        x, y = first_x + jnp.asarray(cell[0]), first_y + jnp.asarray(cell[1])
        return (x >= 0) & (x < grid_x) & (y >= 0) & (y < grid_y)

    allowed = near & inside(key_cells)[:, None] & inside(query_cells)[None, :]
    return jnp.tile(jnp.where(allowed, 0.0, BLOCKED).astype(jnp.float32), (1, GROUP))


def biases(along_x, along_y, depth, first_x, first_y, grid_x, grid_y):
    left_y, own_y, right_y = range(-3, 0), range(along_y), range(along_y, along_y + 3)
    spare = np.full((2, SIDE - 36), -1000)
    core = np.concatenate([cells(range(along_x), ys, depth) for ys in (left_y, own_y, right_y)], axis=1)

    def rim(xs):
        return np.concatenate(
            [cells(xs, own_y, depth), cells(xs, left_y, depth), spare, cells(xs, right_y, depth), spare], axis=1
        )

    lo_x, hi_x = range(-3, 0), range(along_x, along_x + 3)
    place = (first_x, first_y, grid_x, grid_y)
    main = jnp.stack(
        [
            bias_of(np.concatenate([rim(lo_x), core], axis=1), cells(range(4), own_y, depth), *place),
            bias_of(np.concatenate([core, rim(hi_x)], axis=1), cells(range(4, 8), own_y, depth), *place),
        ]
    )

    def half_core(xs):
        return np.concatenate([cells(xs, ys, depth) for ys in (left_y, own_y, right_y)], axis=1)

    far = np.full((2, 16), -1000)
    lo_q = np.concatenate([far, cells(lo_x, own_y, depth)], axis=1)
    hi_q = np.concatenate([cells(hi_x, own_y, depth), far], axis=1)
    rim_bias = jnp.stack(
        [bias_of(half_core(range(4)), lo_q, *place), bias_of(half_core(range(4, 8)), hi_q, *place)]
    )
    return main, rim_bias


def on_device(queries, key_field, value_field, upstream):
    along_x, along_y, depth, features = queries.shape
    head_size = features // HEADS
    width = GROUP * head_size
    groups = HEADS // GROUP
    scale = 1.0 / math.sqrt(head_size)
    rows = along_x * along_y * depth
    main_bias, rim_bias = biases(
        along_x, along_y, depth,
        lax.axis_index("space") * along_x, lax.axis_index("tp") * along_y,
        along_x * lax.axis_size("space"), along_y * lax.axis_size("tp"),
    )

    def rims(a, b, part):
        return jnp.stack([a[part], b[part]]).reshape(2, SIDE, features)

    low, high = slice(0, 3), slice(along_x - 3, along_x)
    rim_lo = shift(rims(key_field, value_field, high), "space", 1)
    rim_hi = shift(rims(key_field, value_field, low), "space", -1)
    pair = jnp.stack([key_field, value_field])
    core_l = shift(pair[:, :, 1:].reshape(2, 96, features), "tp", 1)
    core_r = shift(pair[:, :, :3].reshape(2, 96, features), "tp", -1)
    both = jnp.stack([rim_lo, rim_hi]).reshape(2, 2, 3, along_y, depth, features)
    rim_l = shift(both[:, :, :, 1:].reshape(2, 2, 36, features), "tp", 1)
    rim_r = shift(both[:, :, :, :3].reshape(2, 2, 36, features), "tp", -1)

    qu_hi, qu_lo, _, _ = lax.optimization_barrier(
        (rims(queries, upstream, high), rims(queries, upstream, low), rim_lo, rim_hi)
    )
    ask_lo = shift(qu_hi, "space", 1)
    ask_hi = shift(qu_lo, "space", -1)

    flat = [x.reshape(rows, features) for x in (queries, upstream, key_field, value_field)]

    def block(*lead):
        return pl.BlockSpec(lead + (width,), lambda g: (0,) * len(lead) + (g,))

    def fixed(*shape):
        return pl.BlockSpec(shape, lambda g: (0,) * len(shape))

    def stat():
        return pl.BlockSpec((2, 1, 1, width), lambda g: (0, g, 0, 0))

    def like(*shape, dtype=jnp.float32):
        return jax.ShapeDtypeStruct(shape, dtype)

    bf16 = jnp.bfloat16
    out, grad_q, lse, dots, part_k, part_v = pl.pallas_call(
        lambda *refs: forward_kernel(scale, *refs),
        grid=(groups,),
        in_specs=[block(rows)] * 4
        + [block(2, 96)] * 2
        + [block(2, SIDE)] * 2
        + [block(2, 2, 36)] * 2
        + [fixed(2, SPAN, width)],
        out_specs=[block(rows), block(rows), stat(), stat(), block(CORE), block(CORE)],
        out_shape=[
            like(rows, features, dtype=bf16),
            like(rows, features, dtype=bf16),
            like(2, groups, 1, width),
            like(2, groups, 1, width),
            like(CORE, features),
            like(CORE, features),
        ],
        scratch_shapes=[pltpu.VMEM((FULL, width), bf16), pltpu.VMEM((FULL, width), bf16)],
        compiler_params=pltpu.CompilerParams(
            dimension_semantics=("arbitrary",), vmem_limit_bytes=40 * 1024 * 1024
        ),
        cost_estimate=pl.CostEstimate(flops=4_000_000_000, bytes_accessed=8_000_000, transcendentals=1_000_000),
        name="attend",
    )(*flat, core_l, core_r, rim_lo, rim_hi, rim_l, rim_r, main_bias)

    lse_lo = shift(jnp.stack([lse[1], dots[1]]), "space", 1)
    lse_hi = shift(jnp.stack([lse[0], dots[0]]), "space", -1)

    def one_stat():
        return pl.BlockSpec((1, 1, width), lambda g: (g, 0, 0))

    own, left, right = pl.pallas_call(
        lambda *refs: rim_kernel(scale, *refs),
        grid=(groups,),
        in_specs=[block(2, SIDE)] * 2
        + [one_stat()] * 4
        + [block(rows)] * 2
        + [block(2, 96)] * 2
        + [fixed(2, 160, width)]
        + [block(CORE)] * 2,
        out_specs=[block(2, rows), block(2, 96), block(2, 96)],
        out_shape=[
            like(2, rows, features),
            like(2, 96, features, dtype=bf16),
            like(2, 96, features, dtype=bf16),
        ],
        compiler_params=pltpu.CompilerParams(
            dimension_semantics=("arbitrary",), vmem_limit_bytes=40 * 1024 * 1024
        ),
        cost_estimate=pl.CostEstimate(flops=1_000_000_000, bytes_accessed=5_000_000, transcendentals=300_000),
        name="rims",
    )(
        ask_lo, ask_hi, lse_lo[0], lse_lo[1], lse_hi[0], lse_hi[1], flat[2], flat[3],
        core_l, core_r, rim_bias, part_k, part_v,
    )
    from_next = shift(left, "tp", -1).reshape(2, along_x, 3, depth, features)
    from_prev = shift(right, "tp", 1).reshape(2, along_x, 3, depth, features)
    total = own.reshape(2, along_x, along_y, depth, features)
    edge = [(0, 0)] * 5
    first, last = list(edge), list(edge)
    first[2], last[2] = (0, along_y - 3), (along_y - 3, 0)
    total = total + jnp.pad(from_prev, first) + jnp.pad(from_next, last)
    grads = total.astype(bf16)
    shape_out = (along_x, along_y, depth, features)
    return out.reshape(shape_out), grad_q.reshape(shape_out), grads[0], grads[1]


def solution(mesh):
    spec = P("space", "tp", None, None)
    return jax.shard_map(
        on_device, mesh=mesh, in_specs=(spec,) * 4, out_specs=(spec,) * 4, check_vma=False
    )
```

```python
import math

import jax
import jax.numpy as jnp
from jax import lax
from jax.experimental import pallas as pl
from jax.experimental.pallas import tpu as pltpu
from jax.sharding import PartitionSpec as P

HEADS = 16
RADIUS = 3
BLOCKED = -1e30

GROUP = 4
SIDE = 48
RIM = 3 * SIDE
CORE = 320
SPAN = CORE + RIM
FULL = CORE + 2 * RIM


def by_contract(a, b, dims):
    return lax.dot_general(a, b, (dims, ((), ())), preferred_element_type=jnp.float32)


def shift(x, axis, by):
    peers = lax.axis_size(axis)
    pairs = [(i, i + by) for i in range(peers) if 0 <= i + by < peers]
    return lax.ppermute(x, axis, pairs)


def flat(x):
    return x.reshape(-1, x.shape[-1])


def shaped(x, ref):
    return x.astype(ref.dtype).reshape(ref.shape)


def heads_of(bias):
    return jnp.concatenate([bias, bias], axis=1)


def block_diagonal(rows, scale=None):
    count, width = rows.shape
    if scale is not None:
        rows = rows * jnp.asarray(scale, rows.dtype)
    tiled = jnp.concatenate([rows] * GROUP, axis=0)
    own = lax.broadcasted_iota(jnp.int32, tiled.shape, 0) // count
    head = lax.broadcasted_iota(jnp.int32, tiled.shape, 1) // (width // GROUP)
    return jnp.where(own == head, tiled, jnp.zeros_like(tiled))


def diagonal_of(product, count):
    width = product.shape[1]
    head = lax.broadcasted_iota(jnp.int32, (count, width), 1) // (width // GROUP)
    total = product[0:count]
    for h in range(1, GROUP):
        total = jnp.where(head == h, product[h * count : (h + 1) * count], total)
    return total


def in_three(x):
    first = x.astype(jnp.bfloat16)
    rest = x - first.astype(jnp.float32)
    second = rest.astype(jnp.bfloat16)
    third = (rest - second.astype(jnp.float32)).astype(jnp.bfloat16)
    return [first, second, third]


def score_kernel(
    scale,
    q_ref, u_ref, k_ref, v_ref, cl_ref, cr_ref, rlo_ref, rhi_ref, rl_ref, rr_ref, bias_ref,
    weight_ref, dscore_ref, keys_ref, vals_ref, send_l_ref, send_r_ref,
):
    width = q_ref.shape[-1]
    spare = jnp.zeros((SIDE - 36, width), jnp.bfloat16)
    for buf, own, part in ((keys_ref, k_ref, 0), (vals_ref, v_ref, 1)):
        buf[RIM : RIM + 96] = flat(cl_ref[part])
        buf[RIM + 96 : RIM + 224] = flat(own[...])
        buf[RIM + 224 : RIM + 320] = flat(cr_ref[part])
        for side, rim_ref in ((0, rlo_ref), (1, rhi_ref)):
            base = side * (RIM + CORE)
            buf[base : base + SIDE] = flat(rim_ref[part])
            for at, far_ref in ((base + SIDE, rl_ref), (base + 2 * SIDE, rr_ref)):
                buf[at : at + SIDE] = jnp.concatenate([flat(far_ref[side, part]), spare], axis=0)

    for half, send_ref in ((1, send_r_ref), (0, send_l_ref)):
        keys = keys_ref[half * RIM : half * RIM + SPAN]
        vals = vals_ref[half * RIM : half * RIM + SPAN]
        cell = slice(4 * half, 4 * half + 4)
        query = block_diagonal(flat(q_ref[cell]), scale)
        up = block_diagonal(flat(u_ref[cell]))
        scores = by_contract(keys, query, ((1,), (1,))) + heads_of(bias_ref[half])
        highest = jnp.max(scores, axis=0, keepdims=True)
        prob = jnp.exp(scores - highest)
        summed = jnp.sum(prob, axis=0, keepdims=True)
        prob = prob * (1.0 / summed)
        weights = prob.astype(jnp.bfloat16)
        weight_ref[half] = weights
        d_prob = by_contract(vals, up, ((1,), (1,)))
        dots = jnp.sum(weights.astype(jnp.float32) * d_prob, axis=0, keepdims=True)
        dscore_ref[half] = (prob * (d_prob - dots)).astype(jnp.bfloat16)
        edge = slice(5, 8) if half else slice(0, 3)
        send_ref[0:12] = q_ref[edge].reshape(12, 4, width)
        send_ref[12:24] = u_ref[edge].reshape(12, 4, width)
        rows = in_three(highest + jnp.log(summed)) + in_three(dots)
        rows = jnp.concatenate([x.astype(jnp.float32) for x in rows + rows[:2]], axis=0)
        send_ref[24:26] = shaped(rows, send_ref.at[24:26])


def value_kernel(
    scale,
    weight_ref, dscore_ref, keys_ref, vals_ref, q_ref, u_ref,
    out_ref, dq_ref, dk_ref, dv_ref,
):
    for half in range(2):
        keys = keys_ref[half * RIM : half * RIM + SPAN]
        vals = vals_ref[half * RIM : half * RIM + SPAN]
        cell = slice(4 * half, 4 * half + 4)
        first = RIM * (1 - half)
        query = block_diagonal(flat(q_ref[cell]), scale)
        up = block_diagonal(flat(u_ref[cell]))
        out = by_contract(weight_ref[half], vals, ((0,), (0,)))
        out_ref[cell] = shaped(diagonal_of(out, 64), out_ref.at[cell])
        grad_q = by_contract(dscore_ref[half], keys, ((0,), (0,)))
        dq_ref[cell] = shaped(diagonal_of(grad_q, 64) * scale, dq_ref.at[cell])
        part_k = by_contract(dscore_ref[half, first : first + CORE], query, ((1,), (0,)))
        part_v = by_contract(weight_ref[half, first : first + CORE], up, ((1,), (0,)))
        if half == 0:
            dk_ref[...] = part_k
            dv_ref[...] = part_v
        else:
            dk_ref[...] += part_k
            dv_ref[...] += part_v


def rim_kernel(
    scale,
    asklo_ref, askhi_ref, k_ref, v_ref, cl_ref, cr_ref, bias_ref, dk_ref, dv_ref,
    own_ref, left_ref, right_ref,
):
    for side, ask_ref in enumerate((asklo_ref, askhi_ref)):
        cell = slice(4 * side, 4 * side + 4)
        keys = jnp.concatenate([flat(x) for x in (cl_ref[0, cell], k_ref[cell], cr_ref[0, cell])], axis=0)
        vals = jnp.concatenate([flat(x) for x in (cl_ref[1, cell], v_ref[cell], cr_ref[1, cell])], axis=0)
        blank = jnp.zeros((16, keys.shape[1]), jnp.bfloat16)
        order = (lambda x: [blank, x]) if side == 0 else (lambda x: [x, blank])
        query = block_diagonal(jnp.concatenate(order(flat(ask_ref[0:12])), axis=0), scale)
        up = block_diagonal(jnp.concatenate(order(flat(ask_ref[12:24])), axis=0))
        scores = by_contract(keys, query, ((1,), (1,))) + heads_of(bias_ref[side])
        stat = flat(ask_ref[24:26]).astype(jnp.float32)
        lse = stat[0:1] + stat[1:2] + stat[2:3]
        dots = stat[3:4] + stat[4:5] + stat[5:6]
        prob = jnp.exp(scores - lse)
        weights = prob.astype(jnp.bfloat16)
        d_prob = by_contract(vals, up, ((1,), (1,)))
        d_score = (prob * (d_prob - dots)).astype(jnp.bfloat16)
        parts = (
            (0, dk_ref, by_contract(d_score, query, ((1,), (0,)))),
            (1, dv_ref, by_contract(weights, up, ((1,), (0,)))),
        )
        for which, sum_ref, extra in parts:
            left = slice(48 * side, 48 * side + 48)
            mid = slice(96 + 64 * side, 160 + 64 * side)
            right = slice(224 + 48 * side, 272 + 48 * side)
            left_ref[which, cell] = shaped(sum_ref[left] + extra[0:48], left_ref.at[which, cell])
            own_ref[which, cell] = shaped(sum_ref[mid] + extra[48:112], own_ref.at[which, cell])
            right_ref[which, cell] = shaped(sum_ref[right] + extra[112:160], right_ref.at[which, cell])


def fold_kernel(own_ref, next_ref, prev_ref, gk_ref, gv_ref):
    along_y = own_ref.shape[2]
    for which, grad_ref in ((0, gk_ref), (1, gv_ref)):
        for y in range(along_y):
            total = own_ref[which, :, y]
            if y > 0:
                total = total + next_ref[which, :, y - 1].astype(jnp.float32)
            if y < 3:
                total = total + prev_ref[which, :, y].astype(jnp.float32)
            grad_ref[:, y] = total.astype(jnp.bfloat16)


def piece(count, per_x, many_x, first_x, first_y):
    row = lax.broadcasted_iota(jnp.int32, (count, 128), 0)
    x = (row * (65536 // per_x + 1)) >> 16
    y = (row - x * per_x) >> 2
    return jnp.where(x < many_x, x + first_x, -1000), y + first_y


def bias_kernel(place_ref, main_ref, rim_ref):
    first_x, first_y, grid_x, grid_y = (place_ref[i] for i in range(4))

    def emit(ref, side, at, count, per_x, many_x, x0, y0, query_x0, query_low, query_high):
        lane = lax.broadcasted_iota(jnp.int32, (count, 128), 1) & 63
        qx = query_x0 + (lane >> 4)
        qy = (lane >> 2) & 3
        kx, ky = piece(count, per_x, many_x, x0, y0)
        near = (jnp.abs(kx - qx) <= RADIUS) & (jnp.abs(ky - qy) <= RADIUS)
        gx, gy, hx = kx + first_x, ky + first_y, qx + first_x
        inside = (gx >= 0) & (gx < grid_x) & (gy >= 0) & (gy < grid_y) & (hx >= 0) & (hx < grid_x)
        wanted = (qx >= query_low) & (qx < query_high)
        ref[side, at : at + count] = jnp.where(near & inside & wanted, 0.0, BLOCKED)

    for side in range(2):
        base, first = side * CORE, RIM * (1 - side)
        q0 = 4 * side
        rim_x = -3 if side == 0 else 8
        emit(main_ref, side, base, SIDE, 16, 3, rim_x, 0, q0, 0, 8)
        emit(main_ref, side, base + SIDE, SIDE, 12, 3, rim_x, -3, q0, 0, 8)
        emit(main_ref, side, base + 2 * SIDE, SIDE, 12, 3, rim_x, 4, q0, 0, 8)
        emit(main_ref, side, first, 96, 12, 8, 0, -3, q0, 0, 8)
        emit(main_ref, side, first + 96, 128, 16, 8, 0, 0, q0, 0, 8)
        emit(main_ref, side, first + 224, 96, 12, 8, 0, 4, q0, 0, 8)
        q0, low, high = (-4, -3, 0) if side == 0 else (8, 8, 11)
        emit(rim_ref, side, 0, 48, 12, 4, 4 * side, -3, q0, low, high)
        emit(rim_ref, side, 48, 64, 16, 4, 4 * side, 0, q0, low, high)
        emit(rim_ref, side, 112, 48, 12, 4, 4 * side, 4, q0, low, high)


def on_device(queries, key_field, value_field, upstream):
    along_x, along_y, depth, features = queries.shape
    head_size = features // HEADS
    width = GROUP * head_size
    groups = HEADS // GROUP
    scale = 1.0 / math.sqrt(head_size)
    bf16 = jnp.bfloat16

    def block(*lead):
        return pl.BlockSpec(lead + (width,), lambda g: (0,) * len(lead) + (g,))

    def fixed(*shape):
        return pl.BlockSpec(shape, lambda g: (0,) * len(shape))

    def like(*shape, dtype=jnp.float32):
        return jax.ShapeDtypeStruct(shape, dtype)

    def params(megabytes):
        return pltpu.CompilerParams(
            dimension_semantics=("arbitrary",), vmem_limit_bytes=megabytes * 1024 * 1024
        )

    place = jnp.stack(
        [
            lax.axis_index("space") * along_x,
            lax.axis_index("tp") * along_y,
            jnp.int32(along_x * lax.axis_size("space")),
            jnp.int32(along_y * lax.axis_size("tp")),
        ]
    ).astype(jnp.int32)
    main_bias, rim_bias = pl.pallas_call(
        bias_kernel,
        in_specs=[pl.BlockSpec(memory_space=pltpu.SMEM)],
        out_shape=[like(2, SPAN, 128), like(2, 160, 128)],
        name="masks",
    )(place)

    low, high = slice(0, 3), slice(along_x - 3, along_x)

    def rims(a, b, part):
        return jnp.stack([a[part], b[part]])

    rim_lo = shift(rims(key_field, value_field, high), "space", 1)
    rim_hi = shift(rims(key_field, value_field, low), "space", -1)
    core_l = shift(jnp.stack([key_field[:, 1:], value_field[:, 1:]]), "tp", 1)
    core_r = shift(jnp.stack([key_field[:, :3], value_field[:, :3]]), "tp", -1)
    rim_lo, rim_hi, main_bias, rim_bias = lax.optimization_barrier((rim_lo, rim_hi, main_bias, rim_bias))
    rim_l = shift(jnp.stack([rim_lo[:, :, 1:], rim_hi[:, :, 1:]]), "tp", 1)
    rim_r = shift(jnp.stack([rim_lo[:, :, :3], rim_hi[:, :, :3]]), "tp", -1)

    cells = (along_x, along_y, depth)
    sides = (2, along_x, 3, depth)
    weights, d_score, keys, vals, send_l, send_r = pl.pallas_call(
        lambda *refs: score_kernel(scale, *refs),
        grid=(groups,),
        in_specs=[block(*cells)] * 4
        + [block(*sides)] * 2
        + [block(2, 3, along_y, depth)] * 2
        + [block(2, 2, 3, 3, depth)] * 2
        + [fixed(2, SPAN, 128)],
        out_specs=[block(2, SPAN)] * 2 + [block(FULL)] * 2 + [block(26, depth)] * 2,
        out_shape=[like(2, SPAN, features, dtype=bf16)] * 2
        + [like(FULL, features, dtype=bf16)] * 2
        + [like(26, depth, features, dtype=bf16)] * 2,
        compiler_params=params(40),
        cost_estimate=pl.CostEstimate(flops=1_000_000, bytes_accessed=1_000_000, transcendentals=0),
        name="scores",
    )(queries, upstream, key_field, value_field, core_l, core_r, rim_lo, rim_hi, rim_l, rim_r, main_bias)

    ask_lo = shift(send_r, "space", 1)
    ask_hi = shift(send_l, "space", -1)
    out, grad_q, part_k, part_v = pl.pallas_call(
        lambda *refs: value_kernel(scale, *refs),
        grid=(groups,),
        in_specs=[block(2, SPAN)] * 2 + [block(FULL)] * 2 + [block(*cells)] * 2,
        out_specs=[block(*cells)] * 2 + [block(CORE)] * 2,
        out_shape=[like(*cells, features, dtype=bf16)] * 2 + [like(CORE, features)] * 2,
        compiler_params=params(40),
        cost_estimate=pl.CostEstimate(flops=1_000_000_000, bytes_accessed=8_000_000, transcendentals=0),
        name="values",
    )(weights, d_score, keys, vals, queries, upstream)
    own, left, right = pl.pallas_call(
        lambda *refs: rim_kernel(scale, *refs),
        grid=(groups,),
        in_specs=[block(26, depth)] * 2
        + [block(*cells)] * 2
        + [block(*sides)] * 2
        + [fixed(2, 160, 128)]
        + [block(CORE)] * 2,
        out_specs=[block(2, *cells), block(*sides), block(*sides)],
        out_shape=[
            like(2, *cells, features),
            like(*sides, features, dtype=bf16),
            like(*sides, features, dtype=bf16),
        ],
        compiler_params=params(40),
        cost_estimate=pl.CostEstimate(flops=1_000_000, bytes_accessed=1_000_000, transcendentals=0),
        name="rims",
    )(ask_lo, ask_hi, key_field, value_field, core_l, core_r, rim_bias, part_k, part_v)
    from_next = shift(left, "tp", -1)
    from_prev = shift(right, "tp", 1)
    grad_k, grad_v = pl.pallas_call(
        fold_kernel,
        grid=(groups,),
        in_specs=[block(2, *cells), block(*sides), block(*sides)],
        out_specs=[block(*cells), block(*cells)],
        out_shape=[like(*cells, features, dtype=bf16)] * 2,
        compiler_params=params(40),
        name="fold",
    )(own, from_next, from_prev)
    return out, grad_q, grad_k, grad_v


def solution(mesh):
    spec = P("space", "tp", None, None)
    return jax.shard_map(
        on_device, mesh=mesh, in_specs=(spec,) * 4, out_specs=(spec,) * 4, check_vma=False
    )
```

```python
import math

import jax
import jax.numpy as jnp
from jax import lax
from jax.experimental import pallas as pl
from jax.experimental.pallas import tpu as pltpu
from jax.sharding import PartitionSpec as P

HEADS = 16
RADIUS = 3
BLOCKED = -1e30

GROUP = 4
SIDE = 48
RIM = 3 * SIDE
CORE = 320
SPAN = CORE + RIM


def by_contract(a, b, dims):
    return lax.dot_general(a, b, (dims, ((), ())), preferred_element_type=jnp.float32)


def shift(x, axis, by):
    peers = lax.axis_size(axis)
    pairs = [(i, i + by) for i in range(peers) if 0 <= i + by < peers]
    return lax.ppermute(x, axis, pairs)


def flat(x):
    return x.reshape(-1, x.shape[-1])


def shaped(x, ref):
    return x.astype(ref.dtype).reshape(ref.shape)


def heads_of(bias):
    return jnp.concatenate([bias, bias], axis=1)


def block_diagonal(rows, scale=None):
    count, width = rows.shape
    if scale is not None:
        rows = rows * jnp.asarray(scale, rows.dtype)
    tiled = jnp.concatenate([rows] * GROUP, axis=0)
    own = lax.broadcasted_iota(jnp.int32, tiled.shape, 0) // count
    head = lax.broadcasted_iota(jnp.int32, tiled.shape, 1) // (width // GROUP)
    return jnp.where(own == head, tiled, jnp.zeros_like(tiled))


def diagonal_of(product, count):
    width = product.shape[1]
    head = lax.broadcasted_iota(jnp.int32, (count, width), 1) // (width // GROUP)
    total = product[0:count]
    for h in range(1, GROUP):
        total = jnp.where(head == h, product[h * count : (h + 1) * count], total)
    return total


def in_three(x):
    first = x.astype(jnp.bfloat16)
    rest = x - first.astype(jnp.float32)
    second = rest.astype(jnp.bfloat16)
    third = (rest - second.astype(jnp.float32)).astype(jnp.bfloat16)
    return [first, second, third]


def core_kernel(
    scale,
    q_ref, u_ref, k_ref, v_ref, cl_ref, cr_ref, bias_ref,
    exp_ref, dprob_ref, high_ref, keys_ref, vals_ref,
):
    for buf, own, part in ((keys_ref, k_ref, 0), (vals_ref, v_ref, 1)):
        buf[0:96] = flat(cl_ref[part])
        buf[96:224] = flat(own[...])
        buf[224:320] = flat(cr_ref[part])
    for half in range(2):
        cell = slice(4 * half, 4 * half + 4)
        query = block_diagonal(flat(q_ref[cell]), scale)
        up = block_diagonal(flat(u_ref[cell]))
        scores = by_contract(keys_ref[...], query, ((1,), (1,))) + heads_of(bias_ref[half])
        highest = jnp.max(scores, axis=0, keepdims=True)
        exp_ref[half] = jnp.exp(scores - highest)
        high_ref[half, 0] = highest
        dprob_ref[half] = by_contract(vals_ref[...], up, ((1,), (1,)))


def score_kernel(
    scale,
    exp_ref, dprob_ref, high_ref, q_ref, u_ref, rlo_ref, rhi_ref, rl_ref, rr_ref, bias_ref,
    weight_ref, dscore_ref, keys_ref, vals_ref, odd_ref, terms_ref,
):
    odd = lax.axis_index("space") % 2
    width = q_ref.shape[-1]
    edge = pl.ds(odd * 5, 3)
    odd_ref[0:12] = q_ref[edge].reshape(12, 4, width)
    odd_ref[12:24] = u_ref[edge].reshape(12, 4, width)
    spare = jnp.zeros((SIDE - 36, width), jnp.bfloat16)
    for half, rim_ref in ((0, rlo_ref), (1, rhi_ref)):
        for buf, part in ((keys_ref, 0), (vals_ref, 1)):
            buf[half, 0:SIDE] = flat(rim_ref[part])
            for at, far_ref in ((SIDE, rl_ref), (2 * SIDE, rr_ref)):
                buf[half, at : at + SIDE] = jnp.concatenate([flat(far_ref[half, part]), spare], axis=0)
        cell = slice(4 * half, 4 * half + 4)
        query = block_diagonal(flat(q_ref[cell]), scale)
        up = block_diagonal(flat(u_ref[cell]))
        scores = by_contract(keys_ref[half], query, ((1,), (1,))) + heads_of(bias_ref[half])
        d_prob = by_contract(vals_ref[half], up, ((1,), (1,)))
        before = high_ref[half, 0]
        highest = jnp.maximum(before, jnp.max(scores, axis=0, keepdims=True))
        lowered = jnp.exp(before - highest)
        prob = jnp.exp(scores - highest)
        core = exp_ref[half]
        summed = jnp.sum(prob, axis=0, keepdims=True) + lowered * jnp.sum(core, axis=0, keepdims=True)
        share = 1.0 / summed
        prob = prob * share
        core = core * (share * lowered)
        weights, core_weights = prob.astype(jnp.bfloat16), core.astype(jnp.bfloat16)
        weight_ref[half, CORE:SPAN] = weights
        weight_ref[half, 0:CORE] = core_weights
        dots = jnp.sum(weights.astype(jnp.float32) * d_prob, axis=0, keepdims=True)
        dots += jnp.sum(core_weights.astype(jnp.float32) * dprob_ref[half], axis=0, keepdims=True)
        dscore_ref[half, CORE:SPAN] = (prob * (d_prob - dots)).astype(jnp.bfloat16)
        dscore_ref[half, 0:CORE] = (core * (dprob_ref[half] - dots)).astype(jnp.bfloat16)
        rows = in_three(highest + jnp.log(summed)) + in_three(dots)
        rows = jnp.concatenate([x.astype(jnp.float32) for x in rows + rows[:2]], axis=0)
        terms_ref[half] = shaped(rows, terms_ref.at[half])
    odd_ref[24:26] = terms_ref[odd]


def value_kernel(
    scale,
    weight_ref, dscore_ref, core_k_ref, core_v_ref, rim_k_ref, rim_v_ref, q_ref, u_ref,
    out_ref, dq_ref, dk_ref, dv_ref,
):
    for half in range(2):
        keys = jnp.concatenate([core_k_ref[...], rim_k_ref[half]], axis=0)
        vals = jnp.concatenate([core_v_ref[...], rim_v_ref[half]], axis=0)
        cell = slice(4 * half, 4 * half + 4)
        query = block_diagonal(flat(q_ref[cell]), scale)
        up = block_diagonal(flat(u_ref[cell]))
        out = by_contract(weight_ref[half], vals, ((0,), (0,)))
        out_ref[cell] = shaped(diagonal_of(out, 64), out_ref.at[cell])
        grad_q = by_contract(dscore_ref[half], keys, ((0,), (0,)))
        dq_ref[cell] = shaped(diagonal_of(grad_q, 64) * scale, dq_ref.at[cell])
        part_k = by_contract(dscore_ref[half, 0:CORE], query, ((1,), (0,)))
        part_v = by_contract(weight_ref[half, 0:CORE], up, ((1,), (0,)))
        if half == 0:
            dk_ref[...] = part_k
            dv_ref[...] = part_v
        else:
            dk_ref[...] += part_k
            dv_ref[...] += part_v


def rim_kernel(
    scale,
    odd_ref, even_ref, terms_ref, k_ref, v_ref, cl_ref, cr_ref, bias_ref, dk_ref, dv_ref,
    own_ref, left_ref, right_ref,
    asks,
):
    odd = lax.axis_index("space") % 2
    asks[odd] = odd_ref[...]
    asks[1 - odd, 0:24] = even_ref[...]
    asks[1 - odd, 24:26] = terms_ref[...]
    for side in range(2):
        ask_ref = asks.at[side]
        cell = slice(4 * side, 4 * side + 4)
        keys = jnp.concatenate([flat(x) for x in (cl_ref[0, cell], k_ref[cell], cr_ref[0, cell])], axis=0)
        vals = jnp.concatenate([flat(x) for x in (cl_ref[1, cell], v_ref[cell], cr_ref[1, cell])], axis=0)
        blank = jnp.zeros((16, keys.shape[1]), jnp.bfloat16)
        order = (lambda x: [blank, x]) if side == 0 else (lambda x: [x, blank])
        query = block_diagonal(jnp.concatenate(order(flat(ask_ref[0:12])), axis=0), scale)
        up = block_diagonal(jnp.concatenate(order(flat(ask_ref[12:24])), axis=0))
        scores = by_contract(keys, query, ((1,), (1,))) + heads_of(bias_ref[side])
        stat = flat(ask_ref[24:26]).astype(jnp.float32)
        lse = stat[0:1] + stat[1:2] + stat[2:3]
        dots = stat[3:4] + stat[4:5] + stat[5:6]
        prob = jnp.exp(scores - lse)
        weights = prob.astype(jnp.bfloat16)
        d_prob = by_contract(vals, up, ((1,), (1,)))
        d_score = (prob * (d_prob - dots)).astype(jnp.bfloat16)
        parts = (
            (0, dk_ref, by_contract(d_score, query, ((1,), (0,)))),
            (1, dv_ref, by_contract(weights, up, ((1,), (0,)))),
        )
        for which, sum_ref, extra in parts:
            left = slice(48 * side, 48 * side + 48)
            mid = slice(96 + 64 * side, 160 + 64 * side)
            right = slice(224 + 48 * side, 272 + 48 * side)
            left_ref[which, cell] = shaped(sum_ref[left] + extra[0:48], left_ref.at[which, cell])
            own_ref[which, cell] = shaped(sum_ref[mid] + extra[48:112], own_ref.at[which, cell])
            right_ref[which, cell] = shaped(sum_ref[right] + extra[112:160], right_ref.at[which, cell])


def fold_kernel(own_ref, next_ref, prev_ref, gk_ref, gv_ref):
    along_y = own_ref.shape[2]
    for which, grad_ref in ((0, gk_ref), (1, gv_ref)):
        for y in range(along_y):
            total = own_ref[which, :, y]
            if y > 0:
                total = total + next_ref[which, :, y - 1].astype(jnp.float32)
            if y < 3:
                total = total + prev_ref[which, :, y].astype(jnp.float32)
            grad_ref[:, y] = total.astype(jnp.bfloat16)


def piece(count, per_x, many_x, first_x, first_y):
    row = lax.broadcasted_iota(jnp.int32, (count, 128), 0)
    x = (row * (65536 // per_x + 1)) >> 16
    y = (row - x * per_x) >> 2
    return jnp.where(x < many_x, x + first_x, -1000), y + first_y


def prepare_kernel(q_ref, u_ref, core_ref, edge_ref, rim_ref, even_ref):
    odd = lax.axis_index("space") % 2
    edge = pl.ds((1 - odd) * 5, 3)
    even_ref[0:12] = q_ref[edge].reshape(12, *even_ref.shape[1:])
    even_ref[12:24] = u_ref[edge].reshape(12, *even_ref.shape[1:])
    first_x, first_y = lax.axis_index("space") * 8, lax.axis_index("tp") * 4
    grid_x, grid_y = lax.axis_size("space") * 8, lax.axis_size("tp") * 4

    def emit(ref, side, at, count, per_x, many_x, x0, y0, query_x0, query_low, query_high):
        lane = lax.broadcasted_iota(jnp.int32, (count, 128), 1) & 63
        qx = query_x0 + (lane >> 4)
        qy = (lane >> 2) & 3
        kx, ky = piece(count, per_x, many_x, x0, y0)
        near = (jnp.abs(kx - qx) <= RADIUS) & (jnp.abs(ky - qy) <= RADIUS)
        gx, gy, hx = kx + first_x, ky + first_y, qx + first_x
        inside = (gx >= 0) & (gx < grid_x) & (gy >= 0) & (gy < grid_y) & (hx >= 0) & (hx < grid_x)
        wanted = (qx >= query_low) & (qx < query_high)
        ref[side, at : at + count] = jnp.where(near & inside & wanted, 0.0, BLOCKED)

    for side in range(2):
        q0 = 4 * side
        edge_x = -3 if side == 0 else 8
        emit(core_ref, side, 0, 96, 12, 8, 0, -3, q0, 0, 8)
        emit(core_ref, side, 96, 128, 16, 8, 0, 0, q0, 0, 8)
        emit(core_ref, side, 224, 96, 12, 8, 0, 4, q0, 0, 8)
        emit(edge_ref, side, 0, SIDE, 16, 3, edge_x, 0, q0, 0, 8)
        emit(edge_ref, side, SIDE, SIDE, 12, 3, edge_x, -3, q0, 0, 8)
        emit(edge_ref, side, 2 * SIDE, SIDE, 12, 3, edge_x, 4, q0, 0, 8)
        q0, low, high = (-4, -3, 0) if side == 0 else (8, 8, 11)
        emit(rim_ref, side, 0, 48, 12, 4, 4 * side, -3, q0, low, high)
        emit(rim_ref, side, 48, 64, 16, 4, 4 * side, 0, q0, low, high)
        emit(rim_ref, side, 112, 48, 12, 4, 4 * side, 4, q0, low, high)


def on_device(queries, key_field, value_field, upstream):
    along_x, along_y, depth, features = queries.shape
    head_size = features // HEADS
    width = GROUP * head_size
    groups = HEADS // GROUP
    scale = 1.0 / math.sqrt(head_size)
    bf16 = jnp.bfloat16

    def block(*lead):
        return pl.BlockSpec(lead + (width,), lambda g: (0,) * len(lead) + (g,))

    def fixed(*shape):
        return pl.BlockSpec(shape, lambda g: (0,) * len(shape))

    def like(*shape, dtype=jnp.float32):
        return jax.ShapeDtypeStruct(shape, dtype)

    def params(megabytes):
        return pltpu.CompilerParams(
            dimension_semantics=("arbitrary",), vmem_limit_bytes=megabytes * 1024 * 1024
        )

    spaces = lax.axis_size("space")
    swaps = [[], []]
    for i in range(spaces - 1):
        swaps[i % 2] += [(i, i + 1), (i + 1, i)]
    core_bias, edge_bias, rim_bias, even_send = pl.pallas_call(
        prepare_kernel,
        out_shape=[like(2, CORE, 128), like(2, RIM, 128), like(2, 160, 128), like(24, depth, features, dtype=bf16)],
        compiler_params=pltpu.CompilerParams(vmem_limit_bytes=12 * 1024 * 1024),
        name="prepare",
    )(queries, upstream)
    low, high = slice(0, 3), slice(along_x - 3, along_x)

    def rims(a, b, part):
        return jnp.stack([a[part], b[part]])

    rim_lo = shift(rims(key_field, value_field, high), "space", 1)
    rim_hi = shift(rims(key_field, value_field, low), "space", -1)
    core_l = shift(jnp.stack([key_field[:, 1:], value_field[:, 1:]]), "tp", 1)
    core_r = shift(jnp.stack([key_field[:, :3], value_field[:, :3]]), "tp", -1)
    rim_lo, rim_hi, core_bias, rim_bias = lax.optimization_barrier((rim_lo, rim_hi, core_bias, rim_bias))
    rim_l = shift(jnp.stack([rim_lo[:, :, 1:], rim_hi[:, :, 1:]]), "tp", 1)
    rim_r = shift(jnp.stack([rim_lo[:, :, :3], rim_hi[:, :, :3]]), "tp", -1)

    cells = (along_x, along_y, depth)
    sides = (2, along_x, 3, depth)
    def per_half():
        return pl.BlockSpec((2, 1, 1, width), lambda g: (0, g, 0, 0))

    light = pl.CostEstimate(flops=1_000_000, bytes_accessed=1_000_000, transcendentals=0)
    exps, d_prob, high, core_k, core_v = pl.pallas_call(
        lambda *refs: core_kernel(scale, *refs),
        grid=(groups,),
        in_specs=[block(*cells)] * 4 + [block(*sides)] * 2 + [fixed(2, CORE, 128)],
        out_specs=[block(2, CORE)] * 2 + [per_half()] + [block(CORE)] * 2,
        out_shape=[like(2, CORE, features)] * 2
        + [like(2, groups, 1, width)]
        + [like(CORE, features, dtype=bf16)] * 2,
        compiler_params=params(24),
        cost_estimate=light,
        name="core",
    )(queries, upstream, key_field, value_field, core_l, core_r, core_bias)
    even_send, high = lax.optimization_barrier((even_send, high))
    ask_even = lax.ppermute(even_send, "space", swaps[0])
    weights, d_score, rim_k, rim_v, odd_send, terms = pl.pallas_call(
        lambda *refs: score_kernel(scale, *refs),
        grid=(groups,),
        in_specs=[block(2, CORE)] * 2
        + [per_half()]
        + [block(*cells)] * 2
        + [block(2, 3, along_y, depth)] * 2
        + [block(2, 2, 3, 3, depth)] * 2
        + [fixed(2, RIM, 128)],
        out_specs=[block(2, SPAN)] * 2 + [block(2, RIM)] * 2 + [block(26, depth), block(2, 2, depth)],
        out_shape=[like(2, SPAN, features, dtype=bf16)] * 2
        + [like(2, RIM, features, dtype=bf16)] * 2
        + [like(26, depth, features, dtype=bf16), like(2, 2, depth, features, dtype=bf16)],
        compiler_params=params(24),
        cost_estimate=light,
        name="scores",
    )(exps, d_prob, high, queries, upstream, rim_lo, rim_hi, rim_l, rim_r, edge_bias)

    ask_odd = lax.ppermute(odd_send, "space", swaps[1])
    odd = lax.axis_index("space") % 2
    terms_even = lax.ppermute(jnp.where(odd == 1, terms[0], terms[1]), "space", swaps[0])
    out, grad_q, part_k, part_v = pl.pallas_call(
        lambda *refs: value_kernel(scale, *refs),
        grid=(groups,),
        in_specs=[block(2, SPAN)] * 2 + [block(CORE)] * 2 + [block(2, RIM)] * 2 + [block(*cells)] * 2,
        out_specs=[block(*cells)] * 2 + [block(CORE)] * 2,
        out_shape=[like(*cells, features, dtype=bf16)] * 2 + [like(CORE, features)] * 2,
        compiler_params=params(24),
        cost_estimate=pl.CostEstimate(flops=1_000_000_000, bytes_accessed=8_000_000, transcendentals=0),
        name="values",
    )(weights, d_score, core_k, core_v, rim_k, rim_v, queries, upstream)
    own, left, right = pl.pallas_call(
        lambda *refs: rim_kernel(scale, *refs),
        grid=(groups,),
        in_specs=[block(26, depth), block(24, depth), block(2, depth)]
        + [block(*cells)] * 2
        + [block(*sides)] * 2
        + [fixed(2, 160, 128)]
        + [block(CORE)] * 2,
        out_specs=[block(2, *cells), block(*sides), block(*sides)],
        out_shape=[
            like(2, *cells, features),
            like(*sides, features, dtype=bf16),
            like(*sides, features, dtype=bf16),
        ],
        compiler_params=params(24),
        cost_estimate=pl.CostEstimate(flops=1_000_000, bytes_accessed=1_000_000, transcendentals=0),
        scratch_shapes=[pltpu.VMEM((2, 26, depth, width), bf16)],
        name="rims",
    )(ask_odd, ask_even, terms_even, key_field, value_field, core_l, core_r, rim_bias, part_k, part_v)
    from_next = shift(left, "tp", -1)
    from_prev = shift(right, "tp", 1)
    grad_k, grad_v = pl.pallas_call(
        fold_kernel,
        grid=(groups,),
        in_specs=[block(2, *cells), block(*sides), block(*sides)],
        out_specs=[block(*cells), block(*cells)],
        out_shape=[like(*cells, features, dtype=bf16)] * 2,
        compiler_params=params(24),
        name="fold",
    )(own, from_next, from_prev)
    return out, grad_q, grad_k, grad_v


def solution(mesh):
    spec = P("space", "tp", None, None)
    return jax.shard_map(
        on_device, mesh=mesh, in_specs=(spec,) * 4, out_specs=(spec,) * 4, check_vma=False
    )
```

```python
import math

import jax
import jax.numpy as jnp
from jax import lax
from jax.experimental import pallas as pl
from jax.experimental.pallas import tpu as pltpu
from jax.sharding import PartitionSpec as P

HEADS = 16
RADIUS = 3
BLOCKED = -1e30

GROUP = 4
SIDE = 48
RIM = 3 * SIDE
CORE = 320
SPAN = CORE + RIM


def by_contract(a, b, dims):
    return lax.dot_general(a, b, (dims, ((), ())), preferred_element_type=jnp.float32)


def shift(x, axis, by):
    peers = lax.axis_size(axis)
    pairs = [(i, i + by) for i in range(peers) if 0 <= i + by < peers]
    return lax.ppermute(x, axis, pairs)


def flat(x):
    return x.reshape(-1, x.shape[-1])


def shaped(x, ref):
    return x.astype(ref.dtype).reshape(ref.shape)


def heads_of(bias):
    return jnp.concatenate([bias, bias], axis=1)


def block_diagonal(rows, scale=None):
    count, width = rows.shape
    if scale is not None:
        rows = rows * jnp.asarray(scale, rows.dtype)
    tiled = jnp.concatenate([rows] * GROUP, axis=0)
    own = lax.broadcasted_iota(jnp.int32, tiled.shape, 0) // count
    head = lax.broadcasted_iota(jnp.int32, tiled.shape, 1) // (width // GROUP)
    return jnp.where(own == head, tiled, jnp.zeros_like(tiled))


def diagonal_of(product, count):
    width = product.shape[1]
    head = lax.broadcasted_iota(jnp.int32, (count, width), 1) // (width // GROUP)
    total = product[0:count]
    for h in range(1, GROUP):
        total = jnp.where(head == h, product[h * count : (h + 1) * count], total)
    return total


def in_three(x):
    first = x.astype(jnp.bfloat16)
    rest = x - first.astype(jnp.float32)
    second = rest.astype(jnp.bfloat16)
    third = (rest - second.astype(jnp.float32)).astype(jnp.bfloat16)
    return [first, second, third]


def each_group(kernel, groups, width):
    def body(*refs):
        for g in range(groups):
            lanes = slice(g * width, (g + 1) * width)
            views = []
            for ref in refs:
                if ref.shape[-1] == groups * width:
                    views.append(ref.at[(slice(None),) * (len(ref.shape) - 1) + (lanes,)])
                elif len(ref.shape) == 4 and ref.shape[1:3] == (groups, 1):
                    views.append(ref.at[:, g : g + 1])
                else:
                    views.append(ref)
            kernel(*views)

    return body


def corner_kernel(lo_ref, hi_ref, last_ref, first_ref):
    for side, rim_ref in enumerate((lo_ref, hi_ref)):
        last_ref[side] = rim_ref[:, :, 1:]
        first_ref[side] = rim_ref[:, :, :3]


def core_kernel(
    scale,
    q_ref, u_ref, k_ref, v_ref, cl_ref, cr_ref, bias_ref,
    exp_ref, dprob_ref, high_ref, keys_ref, vals_ref,
):
    for buf, own, part in ((keys_ref, k_ref, 0), (vals_ref, v_ref, 1)):
        buf[0:96] = flat(cl_ref[part])
        buf[96:224] = flat(own[...])
        buf[224:320] = flat(cr_ref[part])
    for half in range(2):
        cell = slice(4 * half, 4 * half + 4)
        query = block_diagonal(flat(q_ref[cell]), scale)
        up = block_diagonal(flat(u_ref[cell]))
        scores = by_contract(keys_ref[...], query, ((1,), (1,))) + heads_of(bias_ref[half])
        highest = jnp.max(scores, axis=0, keepdims=True)
        exp_ref[half] = jnp.exp(scores - highest)
        high_ref[half, 0] = highest
        dprob_ref[half] = by_contract(vals_ref[...], up, ((1,), (1,)))


def score_kernel(
    scale,
    exp_ref, dprob_ref, high_ref, q_ref, u_ref, rlo_ref, rhi_ref, rl_ref, rr_ref, bias_ref,
    weight_ref, dscore_ref, keys_ref, vals_ref, odd_ref, terms_ref,
):
    odd = lax.axis_index("space") % 2
    width = q_ref.shape[-1]
    edge = pl.ds(odd * 5, 3)
    odd_ref[0:12] = q_ref[edge].reshape(12, 4, width)
    odd_ref[12:24] = u_ref[edge].reshape(12, 4, width)
    spare = jnp.zeros((SIDE - 36, width), jnp.bfloat16)
    for half, rim_ref in ((0, rlo_ref), (1, rhi_ref)):
        for buf, part in ((keys_ref, 0), (vals_ref, 1)):
            buf[half, 0:SIDE] = flat(rim_ref[part])
            for at, far_ref in ((SIDE, rl_ref), (2 * SIDE, rr_ref)):
                buf[half, at : at + SIDE] = jnp.concatenate([flat(far_ref[half, part]), spare], axis=0)
        cell = slice(4 * half, 4 * half + 4)
        query = block_diagonal(flat(q_ref[cell]), scale)
        up = block_diagonal(flat(u_ref[cell]))
        scores = by_contract(keys_ref[half], query, ((1,), (1,))) + heads_of(bias_ref[half])
        d_prob = by_contract(vals_ref[half], up, ((1,), (1,)))
        before = high_ref[half, 0]
        highest = jnp.maximum(before, jnp.max(scores, axis=0, keepdims=True))
        lowered = jnp.exp(before - highest)
        prob = jnp.exp(scores - highest)
        core = exp_ref[half]
        summed = jnp.sum(prob, axis=0, keepdims=True) + lowered * jnp.sum(core, axis=0, keepdims=True)
        share = 1.0 / summed
        prob = prob * share
        core = core * (share * lowered)
        weights, core_weights = prob.astype(jnp.bfloat16), core.astype(jnp.bfloat16)
        weight_ref[half, CORE:SPAN] = weights
        weight_ref[half, 0:CORE] = core_weights
        dots = jnp.sum(weights.astype(jnp.float32) * d_prob, axis=0, keepdims=True)
        dots += jnp.sum(core_weights.astype(jnp.float32) * dprob_ref[half], axis=0, keepdims=True)
        dscore_ref[half, CORE:SPAN] = (prob * (d_prob - dots)).astype(jnp.bfloat16)
        dscore_ref[half, 0:CORE] = (core * (dprob_ref[half] - dots)).astype(jnp.bfloat16)
        rows = in_three(highest + jnp.log(summed)) + in_three(dots)
        rows = jnp.concatenate([x.astype(jnp.float32) for x in rows + rows[:2]], axis=0)
        terms_ref[half] = shaped(rows, terms_ref.at[half])
    odd_ref[24:26] = terms_ref[odd]


def value_kernel(
    scale,
    weight_ref, dscore_ref, core_k_ref, core_v_ref, rim_k_ref, rim_v_ref, q_ref, u_ref,
    out_ref, dq_ref, dk_ref, dv_ref,
):
    for half in range(2):
        keys = jnp.concatenate([core_k_ref[...], rim_k_ref[half]], axis=0)
        vals = jnp.concatenate([core_v_ref[...], rim_v_ref[half]], axis=0)
        cell = slice(4 * half, 4 * half + 4)
        query = block_diagonal(flat(q_ref[cell]), scale)
        up = block_diagonal(flat(u_ref[cell]))
        out = by_contract(weight_ref[half], vals, ((0,), (0,)))
        out_ref[cell] = shaped(diagonal_of(out, 64), out_ref.at[cell])
        grad_q = by_contract(dscore_ref[half], keys, ((0,), (0,)))
        dq_ref[cell] = shaped(diagonal_of(grad_q, 64) * scale, dq_ref.at[cell])
        part_k = by_contract(dscore_ref[half, 0:CORE], query, ((1,), (0,)))
        part_v = by_contract(weight_ref[half, 0:CORE], up, ((1,), (0,)))
        if half == 0:
            dk_ref[...] = part_k
            dv_ref[...] = part_v
        else:
            dk_ref[...] += part_k
            dv_ref[...] += part_v


def rim_kernel(
    scale,
    odd_ref, even_ref, terms_ref, k_ref, v_ref, cl_ref, cr_ref, bias_ref, dk_ref, dv_ref,
    own_ref, left_ref, right_ref,
    asks,
):
    odd = lax.axis_index("space") % 2
    asks[odd] = odd_ref[...]
    asks[1 - odd, 0:24] = even_ref[...]
    asks[1 - odd, 24:26] = terms_ref[...]
    for side in range(2):
        ask_ref = asks.at[side]
        cell = slice(4 * side, 4 * side + 4)
        keys = jnp.concatenate([flat(x) for x in (cl_ref[0, cell], k_ref[cell], cr_ref[0, cell])], axis=0)
        vals = jnp.concatenate([flat(x) for x in (cl_ref[1, cell], v_ref[cell], cr_ref[1, cell])], axis=0)
        blank = jnp.zeros((16, keys.shape[1]), jnp.bfloat16)
        order = (lambda x: [blank, x]) if side == 0 else (lambda x: [x, blank])
        query = block_diagonal(jnp.concatenate(order(flat(ask_ref[0:12])), axis=0), scale)
        up = block_diagonal(jnp.concatenate(order(flat(ask_ref[12:24])), axis=0))
        scores = by_contract(keys, query, ((1,), (1,))) + heads_of(bias_ref[side])
        stat = flat(ask_ref[24:26]).astype(jnp.float32)
        lse = stat[0:1] + stat[1:2] + stat[2:3]
        dots = stat[3:4] + stat[4:5] + stat[5:6]
        prob = jnp.exp(scores - lse)
        weights = prob.astype(jnp.bfloat16)
        d_prob = by_contract(vals, up, ((1,), (1,)))
        d_score = (prob * (d_prob - dots)).astype(jnp.bfloat16)
        parts = (
            (0, dk_ref, by_contract(d_score, query, ((1,), (0,)))),
            (1, dv_ref, by_contract(weights, up, ((1,), (0,)))),
        )
        for which, sum_ref, extra in parts:
            left = slice(48 * side, 48 * side + 48)
            mid = slice(96 + 64 * side, 160 + 64 * side)
            right = slice(224 + 48 * side, 272 + 48 * side)
            left_ref[which, cell] = shaped(sum_ref[left] + extra[0:48], left_ref.at[which, cell])
            own_ref[which, cell] = shaped(sum_ref[mid] + extra[48:112], own_ref.at[which, cell])
            right_ref[which, cell] = shaped(sum_ref[right] + extra[112:160], right_ref.at[which, cell])


def fold_kernel(own_ref, next_ref, prev_ref, gk_ref, gv_ref):
    along_y = own_ref.shape[2]
    for which, grad_ref in ((0, gk_ref), (1, gv_ref)):
        for y in range(along_y):
            total = own_ref[which, :, y]
            if y > 0:
                total = total + next_ref[which, :, y - 1].astype(jnp.float32)
            if y < 3:
                total = total + prev_ref[which, :, y].astype(jnp.float32)
            grad_ref[:, y] = total.astype(jnp.bfloat16)


def piece(count, per_x, many_x, first_x, first_y):
    row = lax.broadcasted_iota(jnp.int32, (count, 128), 0)
    x = (row * (65536 // per_x + 1)) >> 16
    y = (row - x * per_x) >> 2
    return jnp.where(x < many_x, x + first_x, -1000), y + first_y


def prepare_kernel(q_ref, u_ref, core_ref, edge_ref, rim_ref, even_ref):
    odd = lax.axis_index("space") % 2
    edge = pl.ds((1 - odd) * 5, 3)
    even_ref[0:12] = q_ref[edge].reshape(12, *even_ref.shape[1:])
    even_ref[12:24] = u_ref[edge].reshape(12, *even_ref.shape[1:])
    first_x, first_y = lax.axis_index("space") * 8, lax.axis_index("tp") * 4
    grid_x, grid_y = lax.axis_size("space") * 8, lax.axis_size("tp") * 4

    def emit(ref, side, at, count, per_x, many_x, x0, y0, query_x0, query_low, query_high):
        lane = lax.broadcasted_iota(jnp.int32, (count, 128), 1) & 63
        qx = query_x0 + (lane >> 4)
        qy = (lane >> 2) & 3
        kx, ky = piece(count, per_x, many_x, x0, y0)
        near = (jnp.abs(kx - qx) <= RADIUS) & (jnp.abs(ky - qy) <= RADIUS)
        gx, gy, hx = kx + first_x, ky + first_y, qx + first_x
        inside = (gx >= 0) & (gx < grid_x) & (gy >= 0) & (gy < grid_y) & (hx >= 0) & (hx < grid_x)
        wanted = (qx >= query_low) & (qx < query_high)
        ref[side, at : at + count] = jnp.where(near & inside & wanted, 0.0, BLOCKED)

    for side in range(2):
        q0 = 4 * side
        edge_x = -3 if side == 0 else 8
        emit(core_ref, side, 0, 96, 12, 8, 0, -3, q0, 0, 8)
        emit(core_ref, side, 96, 128, 16, 8, 0, 0, q0, 0, 8)
        emit(core_ref, side, 224, 96, 12, 8, 0, 4, q0, 0, 8)
        emit(edge_ref, side, 0, SIDE, 16, 3, edge_x, 0, q0, 0, 8)
        emit(edge_ref, side, SIDE, SIDE, 12, 3, edge_x, -3, q0, 0, 8)
        emit(edge_ref, side, 2 * SIDE, SIDE, 12, 3, edge_x, 4, q0, 0, 8)
        q0, low, high = (-4, -3, 0) if side == 0 else (8, 8, 11)
        emit(rim_ref, side, 0, 48, 12, 4, 4 * side, -3, q0, low, high)
        emit(rim_ref, side, 48, 64, 16, 4, 4 * side, 0, q0, low, high)
        emit(rim_ref, side, 112, 48, 12, 4, 4 * side, 4, q0, low, high)


def on_device(queries, key_field, value_field, upstream):
    along_x, along_y, depth, features = queries.shape
    head_size = features // HEADS
    width = GROUP * head_size
    groups = HEADS // GROUP
    scale = 1.0 / math.sqrt(head_size)
    bf16 = jnp.bfloat16

    def block(*lead):
        return pl.BlockSpec(lead + (width,), lambda g: (0,) * len(lead) + (g,))

    def fixed(*shape):
        return pl.BlockSpec(shape, lambda g: (0,) * len(shape))

    def like(*shape, dtype=jnp.float32):
        return jax.ShapeDtypeStruct(shape, dtype)

    def params(megabytes):
        return pltpu.CompilerParams(
            dimension_semantics=("arbitrary",), vmem_limit_bytes=megabytes * 1024 * 1024
        )

    spaces = lax.axis_size("space")
    swaps = [[], []]
    for i in range(spaces - 1):
        swaps[i % 2] += [(i, i + 1), (i + 1, i)]
    core_bias, edge_bias, rim_bias, even_send = pl.pallas_call(
        prepare_kernel,
        out_shape=[like(2, CORE, 128), like(2, RIM, 128), like(2, 160, 128), like(24, depth, features, dtype=bf16)],
        compiler_params=pltpu.CompilerParams(vmem_limit_bytes=12 * 1024 * 1024),
        name="prepare",
    )(queries, upstream)
    low, high = slice(0, 3), slice(along_x - 3, along_x)

    def rims(a, b, part):
        return jnp.stack([a[part], b[part]])

    rim_lo = shift(rims(key_field, value_field, high), "space", 1)
    rim_hi = shift(rims(key_field, value_field, low), "space", -1)
    core_l = shift(jnp.stack([key_field[:, 1:], value_field[:, 1:]]), "tp", 1)
    core_r = shift(jnp.stack([key_field[:, :3], value_field[:, :3]]), "tp", -1)
    rim_lo, rim_hi, core_bias, rim_bias = lax.optimization_barrier((rim_lo, rim_hi, core_bias, rim_bias))
    last_y, first_y = pl.pallas_call(
        corner_kernel,
        out_shape=[like(2, 2, 3, 3, depth, features, dtype=bf16)] * 2,
        compiler_params=pltpu.CompilerParams(vmem_limit_bytes=6 * 1024 * 1024),
        name="corners",
    )(rim_lo, rim_hi)
    rim_l = shift(last_y, "tp", 1)
    rim_r = shift(first_y, "tp", -1)

    cells = (along_x, along_y, depth)
    sides = (2, along_x, 3, depth)
    def per_half():
        return pl.BlockSpec((2, 1, 1, width), lambda g: (0, g, 0, 0))

    light = pl.CostEstimate(flops=1_000_000, bytes_accessed=1_000_000, transcendentals=0)
    exps, d_prob, high, core_k, core_v = pl.pallas_call(
        each_group(lambda *refs: core_kernel(scale, *refs), groups, width),
        out_shape=[like(2, CORE, features)] * 2
        + [like(2, groups, 1, width)]
        + [like(CORE, features, dtype=bf16)] * 2,
        compiler_params=pltpu.CompilerParams(vmem_limit_bytes=30 * 1024 * 1024),
        cost_estimate=light,
        name="core",
    )(queries, upstream, key_field, value_field, core_l, core_r, core_bias)
    even_send, high = lax.optimization_barrier((even_send, high))
    ask_even = lax.ppermute(even_send, "space", swaps[0])
    weights, d_score, rim_k, rim_v, odd_send, terms = pl.pallas_call(
        each_group(lambda *refs: score_kernel(scale, *refs), groups, width),
        out_shape=[like(2, SPAN, features, dtype=bf16)] * 2
        + [like(2, RIM, features, dtype=bf16)] * 2
        + [like(26, depth, features, dtype=bf16), like(2, 2, depth, features, dtype=bf16)],
        compiler_params=pltpu.CompilerParams(vmem_limit_bytes=30 * 1024 * 1024),
        cost_estimate=light,
        name="scores",
    )(exps, d_prob, high, queries, upstream, rim_lo, rim_hi, rim_l, rim_r, edge_bias)

    ask_odd = lax.ppermute(odd_send, "space", swaps[1])
    odd = lax.axis_index("space") % 2
    terms_even = lax.ppermute(jnp.where(odd == 1, terms[0], terms[1]), "space", swaps[0])
    out, grad_q, part_k, part_v = pl.pallas_call(
        each_group(lambda *refs: value_kernel(scale, *refs), groups, width),
        out_shape=[like(*cells, features, dtype=bf16)] * 2 + [like(CORE, features)] * 2,
        compiler_params=pltpu.CompilerParams(vmem_limit_bytes=30 * 1024 * 1024),
        cost_estimate=pl.CostEstimate(flops=1_000_000_000, bytes_accessed=8_000_000, transcendentals=0),
        name="values",
    )(weights, d_score, core_k, core_v, rim_k, rim_v, queries, upstream)
    own, left, right = pl.pallas_call(
        each_group(lambda *refs: rim_kernel(scale, *refs), groups, width),
        out_shape=[
            like(2, *cells, features),
            like(*sides, features, dtype=bf16),
            like(*sides, features, dtype=bf16),
        ],
        compiler_params=pltpu.CompilerParams(vmem_limit_bytes=30 * 1024 * 1024),
        cost_estimate=pl.CostEstimate(flops=1_000_000, bytes_accessed=1_000_000, transcendentals=0),
        scratch_shapes=[pltpu.VMEM((2, 26, depth, width), bf16)],
        name="rims",
    )(ask_odd, ask_even, terms_even, key_field, value_field, core_l, core_r, rim_bias, part_k, part_v)
    from_next = shift(left, "tp", -1)
    from_prev = shift(right, "tp", 1)
    grad_k, grad_v = pl.pallas_call(
        each_group(fold_kernel, groups, width),
        out_shape=[like(*cells, features, dtype=bf16)] * 2,
        compiler_params=pltpu.CompilerParams(vmem_limit_bytes=30 * 1024 * 1024),
        name="fold",
    )(own, from_next, from_prev)
    return out, grad_q, grad_k, grad_v


def solution(mesh):
    spec = P("space", "tp", None, None)
    return jax.shard_map(
        on_device, mesh=mesh, in_specs=(spec,) * 4, out_specs=(spec,) * 4, check_vma=False
    )
```

```python
import math

import jax
import jax.numpy as jnp
from jax import lax
from jax.experimental import pallas as pl
from jax.experimental.pallas import tpu as pltpu
from jax.sharding import PartitionSpec as P

HEADS = 16
RADIUS = 3
BLOCKED = -1e30

GROUP = 4
SIDE = 48
RIM = 3 * SIDE
CORE = 320
SPAN = CORE + RIM


def by_contract(a, b, dims):
    return lax.dot_general(a, b, (dims, ((), ())), preferred_element_type=jnp.float32)


def shift(x, axis, by):
    peers = lax.axis_size(axis)
    pairs = [(i, i + by) for i in range(peers) if 0 <= i + by < peers]
    return lax.ppermute(x, axis, pairs)


def flat(x):
    return x.reshape(-1, x.shape[-1])


def shaped(x, ref):
    return x.astype(ref.dtype).reshape(ref.shape)


def heads_of(bias):
    return jnp.concatenate([bias, bias], axis=1)


def block_diagonal(rows, scale=None):
    count, width = rows.shape
    if scale is not None:
        rows = rows * jnp.asarray(scale, rows.dtype)
    tiled = jnp.concatenate([rows] * GROUP, axis=0)
    own = lax.broadcasted_iota(jnp.int32, tiled.shape, 0) // count
    head = lax.broadcasted_iota(jnp.int32, tiled.shape, 1) // (width // GROUP)
    return jnp.where(own == head, tiled, jnp.zeros_like(tiled))


def diagonal_of(product, count):
    width = product.shape[1]
    head = lax.broadcasted_iota(jnp.int32, (count, width), 1) // (width // GROUP)
    total = product[0:count]
    for h in range(1, GROUP):
        total = jnp.where(head == h, product[h * count : (h + 1) * count], total)
    return total


def in_three(x):
    first = x.astype(jnp.bfloat16)
    rest = x - first.astype(jnp.float32)
    second = rest.astype(jnp.bfloat16)
    third = (rest - second.astype(jnp.float32)).astype(jnp.bfloat16)
    return [first, second, third]


def each_group(kernel, groups, width):
    def body(*refs):
        for g in range(groups):
            lanes = slice(g * width, (g + 1) * width)
            views = []
            for ref in refs:
                if ref.shape[-1] == groups * width:
                    views.append(ref.at[(slice(None),) * (len(ref.shape) - 1) + (lanes,)])
                elif len(ref.shape) == 4 and ref.shape[1:3] == (groups, 1):
                    views.append(ref.at[:, g : g + 1])
                else:
                    views.append(ref)
            kernel(*views)

    return body


def column_kernel(k_ref, v_ref, last_ref, first_ref):
    for part, own_ref in enumerate((k_ref, v_ref)):
        last_ref[part] = own_ref[:, 1:]
        first_ref[part] = own_ref[:, :3]


def corner_kernel(lo_ref, hi_ref, last_ref, first_ref):
    for side, rim_ref in enumerate((lo_ref, hi_ref)):
        last_ref[side] = rim_ref[:, :, 1:]
        first_ref[side] = rim_ref[:, :, :3]


def core_kernel(
    scale,
    q_ref, u_ref, k_ref, v_ref, cl_ref, cr_ref, bias_ref,
    exp_ref, dprob_ref, high_ref, keys_ref, vals_ref,
):
    for buf, own, part in ((keys_ref, k_ref, 0), (vals_ref, v_ref, 1)):
        buf[0:96] = flat(cl_ref[part])
        buf[96:224] = flat(own[...])
        buf[224:320] = flat(cr_ref[part])
    for half in range(2):
        cell = slice(4 * half, 4 * half + 4)
        query = block_diagonal(flat(q_ref[cell]), scale)
        up = block_diagonal(flat(u_ref[cell]))
        scores = by_contract(keys_ref[...], query, ((1,), (1,))) + heads_of(bias_ref[half])
        highest = jnp.max(scores, axis=0, keepdims=True)
        exp_ref[half] = jnp.exp(scores - highest)
        high_ref[half, 0] = highest
        dprob_ref[half] = by_contract(vals_ref[...], up, ((1,), (1,)))


def score_kernel(
    scale,
    exp_ref, dprob_ref, high_ref, q_ref, u_ref, rlo_ref, rhi_ref, rl_ref, rr_ref, bias_ref,
    weight_ref, dscore_ref, keys_ref, vals_ref, odd_ref, terms_ref,
):
    odd = lax.axis_index("space") % 2
    width = q_ref.shape[-1]
    edge = pl.ds(odd * 5, 3)
    odd_ref[0:12] = q_ref[edge].reshape(12, 4, width)
    odd_ref[12:24] = u_ref[edge].reshape(12, 4, width)
    spare = jnp.zeros((SIDE - 36, width), jnp.bfloat16)
    for half, rim_ref in ((0, rlo_ref), (1, rhi_ref)):
        for buf, part in ((keys_ref, 0), (vals_ref, 1)):
            buf[half, 0:SIDE] = flat(rim_ref[part])
            for at, far_ref in ((SIDE, rl_ref), (2 * SIDE, rr_ref)):
                buf[half, at : at + SIDE] = jnp.concatenate([flat(far_ref[half, part]), spare], axis=0)
        cell = slice(4 * half, 4 * half + 4)
        query = block_diagonal(flat(q_ref[cell]), scale)
        up = block_diagonal(flat(u_ref[cell]))
        scores = by_contract(keys_ref[half], query, ((1,), (1,))) + heads_of(bias_ref[half])
        d_prob = by_contract(vals_ref[half], up, ((1,), (1,)))
        before = high_ref[half, 0]
        highest = jnp.maximum(before, jnp.max(scores, axis=0, keepdims=True))
        lowered = jnp.exp(before - highest)
        prob = jnp.exp(scores - highest)
        core = exp_ref[half]
        summed = jnp.sum(prob, axis=0, keepdims=True) + lowered * jnp.sum(core, axis=0, keepdims=True)
        share = 1.0 / summed
        prob = prob * share
        core = core * (share * lowered)
        weights, core_weights = prob.astype(jnp.bfloat16), core.astype(jnp.bfloat16)
        weight_ref[half, CORE:SPAN] = weights
        weight_ref[half, 0:CORE] = core_weights
        dots = jnp.sum(weights.astype(jnp.float32) * d_prob, axis=0, keepdims=True)
        dots += jnp.sum(core_weights.astype(jnp.float32) * dprob_ref[half], axis=0, keepdims=True)
        dscore_ref[half, CORE:SPAN] = (prob * (d_prob - dots)).astype(jnp.bfloat16)
        dscore_ref[half, 0:CORE] = (core * (dprob_ref[half] - dots)).astype(jnp.bfloat16)
        rows = in_three(highest + jnp.log(summed)) + in_three(dots)
        rows = jnp.concatenate([x.astype(jnp.float32) for x in rows + rows[:2]], axis=0)
        terms_ref[half] = shaped(rows, terms_ref.at[half])
    odd_ref[24:26] = terms_ref[odd]


def value_kernel(
    scale,
    weight_ref, dscore_ref, core_k_ref, core_v_ref, rim_k_ref, rim_v_ref, q_ref, u_ref,
    out_ref, dq_ref, dk_ref, dv_ref,
):
    for half in range(2):
        keys = jnp.concatenate([core_k_ref[...], rim_k_ref[half]], axis=0)
        vals = jnp.concatenate([core_v_ref[...], rim_v_ref[half]], axis=0)
        cell = slice(4 * half, 4 * half + 4)
        query = block_diagonal(flat(q_ref[cell]), scale)
        up = block_diagonal(flat(u_ref[cell]))
        out = by_contract(weight_ref[half], vals, ((0,), (0,)))
        out_ref[cell] = shaped(diagonal_of(out, 64), out_ref.at[cell])
        grad_q = by_contract(dscore_ref[half], keys, ((0,), (0,)))
        dq_ref[cell] = shaped(diagonal_of(grad_q, 64) * scale, dq_ref.at[cell])
        part_k = by_contract(dscore_ref[half, 0:CORE], query, ((1,), (0,)))
        part_v = by_contract(weight_ref[half, 0:CORE], up, ((1,), (0,)))
        if half == 0:
            dk_ref[...] = part_k
            dv_ref[...] = part_v
        else:
            dk_ref[...] += part_k
            dv_ref[...] += part_v


def rim_kernel(
    scale,
    odd_ref, even_ref, terms_ref, k_ref, v_ref, cl_ref, cr_ref, bias_ref, dk_ref, dv_ref,
    own_ref, left_ref, right_ref,
    asks,
):
    odd = lax.axis_index("space") % 2
    asks[odd] = odd_ref[...]
    asks[1 - odd, 0:24] = even_ref[...]
    asks[1 - odd, 24:26] = terms_ref[...]
    for side in range(2):
        ask_ref = asks.at[side]
        cell = slice(4 * side, 4 * side + 4)
        keys = jnp.concatenate([flat(x) for x in (cl_ref[0, cell], k_ref[cell], cr_ref[0, cell])], axis=0)
        vals = jnp.concatenate([flat(x) for x in (cl_ref[1, cell], v_ref[cell], cr_ref[1, cell])], axis=0)
        blank = jnp.zeros((16, keys.shape[1]), jnp.bfloat16)
        order = (lambda x: [blank, x]) if side == 0 else (lambda x: [x, blank])
        query = block_diagonal(jnp.concatenate(order(flat(ask_ref[0:12])), axis=0), scale)
        up = block_diagonal(jnp.concatenate(order(flat(ask_ref[12:24])), axis=0))
        scores = by_contract(keys, query, ((1,), (1,))) + heads_of(bias_ref[side])
        stat = flat(ask_ref[24:26]).astype(jnp.float32)
        lse = stat[0:1] + stat[1:2] + stat[2:3]
        dots = stat[3:4] + stat[4:5] + stat[5:6]
        prob = jnp.exp(scores - lse)
        weights = prob.astype(jnp.bfloat16)
        d_prob = by_contract(vals, up, ((1,), (1,)))
        d_score = (prob * (d_prob - dots)).astype(jnp.bfloat16)
        parts = (
            (0, dk_ref, by_contract(d_score, query, ((1,), (0,)))),
            (1, dv_ref, by_contract(weights, up, ((1,), (0,)))),
        )
        for which, sum_ref, extra in parts:
            left = slice(48 * side, 48 * side + 48)
            mid = slice(96 + 64 * side, 160 + 64 * side)
            right = slice(224 + 48 * side, 272 + 48 * side)
            left_ref[which, cell] = shaped(sum_ref[left] + extra[0:48], left_ref.at[which, cell])
            own_ref[which, cell] = shaped(sum_ref[mid] + extra[48:112], own_ref.at[which, cell])
            right_ref[which, cell] = shaped(sum_ref[right] + extra[112:160], right_ref.at[which, cell])


def fold_kernel(own_ref, next_ref, prev_ref, gk_ref, gv_ref):
    along_y = own_ref.shape[2]
    for which, grad_ref in ((0, gk_ref), (1, gv_ref)):
        for y in range(along_y):
            total = own_ref[which, :, y]
            if y > 0:
                total = total + next_ref[which, :, y - 1].astype(jnp.float32)
            if y < 3:
                total = total + prev_ref[which, :, y].astype(jnp.float32)
            grad_ref[:, y] = total.astype(jnp.bfloat16)


def piece(count, per_x, many_x, first_x, first_y):
    row = lax.broadcasted_iota(jnp.int32, (count, 128), 0)
    x = (row * (65536 // per_x + 1)) >> 16
    y = (row - x * per_x) >> 2
    return jnp.where(x < many_x, x + first_x, -1000), y + first_y


def prepare_kernel(q_ref, u_ref, core_ref, edge_ref, rim_ref, even_ref):
    odd = lax.axis_index("space") % 2
    edge = pl.ds((1 - odd) * 5, 3)
    even_ref[0:12] = q_ref[edge].reshape(12, *even_ref.shape[1:])
    even_ref[12:24] = u_ref[edge].reshape(12, *even_ref.shape[1:])
    first_x, first_y = lax.axis_index("space") * 8, lax.axis_index("tp") * 4
    grid_x, grid_y = lax.axis_size("space") * 8, lax.axis_size("tp") * 4

    def emit(ref, side, at, count, per_x, many_x, x0, y0, query_x0, query_low, query_high):
        lane = lax.broadcasted_iota(jnp.int32, (count, 128), 1) & 63
        qx = query_x0 + (lane >> 4)
        qy = (lane >> 2) & 3
        kx, ky = piece(count, per_x, many_x, x0, y0)
        near = (jnp.abs(kx - qx) <= RADIUS) & (jnp.abs(ky - qy) <= RADIUS)
        gx, gy, hx = kx + first_x, ky + first_y, qx + first_x
        inside = (gx >= 0) & (gx < grid_x) & (gy >= 0) & (gy < grid_y) & (hx >= 0) & (hx < grid_x)
        wanted = (qx >= query_low) & (qx < query_high)
        ref[side, at : at + count] = jnp.where(near & inside & wanted, 0.0, BLOCKED)

    for side in range(2):
        q0 = 4 * side
        edge_x = -3 if side == 0 else 8
        emit(core_ref, side, 0, 96, 12, 8, 0, -3, q0, 0, 8)
        emit(core_ref, side, 96, 128, 16, 8, 0, 0, q0, 0, 8)
        emit(core_ref, side, 224, 96, 12, 8, 0, 4, q0, 0, 8)
        emit(edge_ref, side, 0, SIDE, 16, 3, edge_x, 0, q0, 0, 8)
        emit(edge_ref, side, SIDE, SIDE, 12, 3, edge_x, -3, q0, 0, 8)
        emit(edge_ref, side, 2 * SIDE, SIDE, 12, 3, edge_x, 4, q0, 0, 8)
        q0, low, high = (-4, -3, 0) if side == 0 else (8, 8, 11)
        emit(rim_ref, side, 0, 48, 12, 4, 4 * side, -3, q0, low, high)
        emit(rim_ref, side, 48, 64, 16, 4, 4 * side, 0, q0, low, high)
        emit(rim_ref, side, 112, 48, 12, 4, 4 * side, 4, q0, low, high)


def on_device(queries, key_field, value_field, upstream):
    along_x, along_y, depth, features = queries.shape
    head_size = features // HEADS
    width = GROUP * head_size
    groups = HEADS // GROUP
    scale = 1.0 / math.sqrt(head_size)
    bf16 = jnp.bfloat16

    def block(*lead):
        return pl.BlockSpec(lead + (width,), lambda g: (0,) * len(lead) + (g,))

    def fixed(*shape):
        return pl.BlockSpec(shape, lambda g: (0,) * len(shape))

    def like(*shape, dtype=jnp.float32):
        return jax.ShapeDtypeStruct(shape, dtype)

    def params(megabytes):
        return pltpu.CompilerParams(
            dimension_semantics=("arbitrary",), vmem_limit_bytes=megabytes * 1024 * 1024
        )

    spaces = lax.axis_size("space")
    swaps = [[], []]
    for i in range(spaces - 1):
        swaps[i % 2] += [(i, i + 1), (i + 1, i)]
    core_bias, edge_bias, rim_bias, even_send = pl.pallas_call(
        prepare_kernel,
        out_shape=[like(2, CORE, 128), like(2, RIM, 128), like(2, 160, 128), like(24, depth, features, dtype=bf16)],
        compiler_params=pltpu.CompilerParams(vmem_limit_bytes=12 * 1024 * 1024),
        name="prepare",
    )(queries, upstream)
    low, high = slice(0, 3), slice(along_x - 3, along_x)

    def rims(a, b, part):
        return jnp.stack([a[part], b[part]])

    rim_lo = shift(rims(key_field, value_field, high), "space", 1)
    rim_hi = shift(rims(key_field, value_field, low), "space", -1)
    last_y, first_y = pl.pallas_call(
        column_kernel,
        out_shape=[like(2, along_x, 3, depth, features, dtype=bf16)] * 2,
        compiler_params=pltpu.CompilerParams(vmem_limit_bytes=6 * 1024 * 1024),
        name="columns",
    )(key_field, value_field)
    core_l = shift(last_y, "tp", 1)
    core_r = shift(first_y, "tp", -1)
    rim_lo, rim_hi, core_bias, rim_bias = lax.optimization_barrier((rim_lo, rim_hi, core_bias, rim_bias))
    last_y, first_y = pl.pallas_call(
        corner_kernel,
        out_shape=[like(2, 2, 3, 3, depth, features, dtype=bf16)] * 2,
        compiler_params=pltpu.CompilerParams(vmem_limit_bytes=6 * 1024 * 1024),
        name="corners",
    )(rim_lo, rim_hi)
    rim_l = shift(last_y, "tp", 1)
    rim_r = shift(first_y, "tp", -1)

    cells = (along_x, along_y, depth)
    sides = (2, along_x, 3, depth)
    def per_half():
        return pl.BlockSpec((2, 1, 1, width), lambda g: (0, g, 0, 0))

    light = pl.CostEstimate(flops=1_000_000, bytes_accessed=1_000_000, transcendentals=0)
    exps, d_prob, high, core_k, core_v = pl.pallas_call(
        each_group(lambda *refs: core_kernel(scale, *refs), groups, width),
        out_shape=[like(2, CORE, features)] * 2
        + [like(2, groups, 1, width)]
        + [like(CORE, features, dtype=bf16)] * 2,
        compiler_params=pltpu.CompilerParams(vmem_limit_bytes=30 * 1024 * 1024),
        cost_estimate=light,
        name="core",
    )(queries, upstream, key_field, value_field, core_l, core_r, core_bias)
    even_send, high = lax.optimization_barrier((even_send, high))
    ask_even = lax.ppermute(even_send, "space", swaps[0])
    weights, d_score, rim_k, rim_v, odd_send, terms = pl.pallas_call(
        each_group(lambda *refs: score_kernel(scale, *refs), groups, width),
        out_shape=[like(2, SPAN, features, dtype=bf16)] * 2
        + [like(2, RIM, features, dtype=bf16)] * 2
        + [like(26, depth, features, dtype=bf16), like(2, 2, depth, features, dtype=bf16)],
        compiler_params=pltpu.CompilerParams(vmem_limit_bytes=30 * 1024 * 1024),
        cost_estimate=light,
        name="scores",
    )(exps, d_prob, high, queries, upstream, rim_lo, rim_hi, rim_l, rim_r, edge_bias)

    ask_odd = lax.ppermute(odd_send, "space", swaps[1])
    odd = lax.axis_index("space") % 2
    terms_even = lax.ppermute(jnp.where(odd == 1, terms[0], terms[1]), "space", swaps[0])
    out, grad_q, part_k, part_v = pl.pallas_call(
        each_group(lambda *refs: value_kernel(scale, *refs), groups, width),
        out_shape=[like(*cells, features, dtype=bf16)] * 2 + [like(CORE, features)] * 2,
        compiler_params=pltpu.CompilerParams(vmem_limit_bytes=30 * 1024 * 1024),
        cost_estimate=pl.CostEstimate(flops=1_000_000_000, bytes_accessed=8_000_000, transcendentals=0),
        name="values",
    )(weights, d_score, core_k, core_v, rim_k, rim_v, queries, upstream)
    own, left, right = pl.pallas_call(
        each_group(lambda *refs: rim_kernel(scale, *refs), groups, width),
        out_shape=[
            like(2, *cells, features),
            like(*sides, features, dtype=bf16),
            like(*sides, features, dtype=bf16),
        ],
        compiler_params=pltpu.CompilerParams(vmem_limit_bytes=30 * 1024 * 1024),
        cost_estimate=pl.CostEstimate(flops=1_000_000, bytes_accessed=1_000_000, transcendentals=0),
        scratch_shapes=[pltpu.VMEM((2, 26, depth, width), bf16)],
        name="rims",
    )(ask_odd, ask_even, terms_even, key_field, value_field, core_l, core_r, rim_bias, part_k, part_v)
    from_next = shift(left, "tp", -1)
    from_prev = shift(right, "tp", 1)
    grad_k, grad_v = pl.pallas_call(
        each_group(fold_kernel, groups, width),
        out_shape=[like(*cells, features, dtype=bf16)] * 2,
        compiler_params=pltpu.CompilerParams(vmem_limit_bytes=30 * 1024 * 1024),
        name="fold",
    )(own, from_next, from_prev)
    return out, grad_q, grad_k, grad_v


def solution(mesh):
    spec = P("space", "tp", None, None)
    return jax.shard_map(
        on_device, mesh=mesh, in_specs=(spec,) * 4, out_specs=(spec,) * 4, check_vma=False
    )
```
